512 devices in a mesh: ctx: 128 (over z, y, core), head: 4 (over x).
Axes of the slice: x: 4, y: 4, z: 16, core: 2. Of those that a mesh axis runs over, the one named last changes fastest.
Arguments:
- queries: bfloat16 [16384, 32, 128], P('ctx', 'head'), may hold values from -22 to 22
- key_states: bfloat16 [16384, 8, 128], P('ctx'), may hold values from -22 to 22
- value_states: bfloat16 [16384, 8, 128], P('ctx'), may hold values from -5 to 5
- grad_out: bfloat16 [16384, 32, 128], P('ctx', 'head'), may hold values from -5 to 5
- selected: int32 [256, 32, 3], P(None, 'head'), may hold values from 0 to 255, as said below
Outputs:
- attention_out: bfloat16 [16384, 32, 128], P('ctx', 'head')
- query_grad: bfloat16 [16384, 32, 128], P('ctx', 'head')
- key_grad: bfloat16 [16384, 8, 128], P('ctx', 'head')
- value_grad: bfloat16 [16384, 8, 128], P('ctx', 'head')
The draws below stay inside these ranges and needn't reach their ends.
Inputs may be any that keep to these rules, and one draw needn't show every extreme that they name: `selected`: for every ctx shard s and head group g, the 48 entries of blocks s * 2 to (s + 1) * 2 - 1 and the group's 8 heads name only blocks of other shards, no shard more than 1 times and some shard exactly 1 times; the 3 entries of one block and head name blocks of different shards.
All inputs are finite; a program needn't handle non-finite values.
Results may differ from the reference program's by a relative error of at most 0.03.
Values may be sent and summed in bfloat16 or wider, within the bound.
A program may use at most 64 MiB of HBM per device.

```python
import jax
import jax.numpy as jnp
from jax import lax

HEAD = 128
QHEADS = 32
KV_HEADS = 8
BLOCK = 64
TOPK = 3
BLK_DEV = 2
QH_DEV = 8
NBLK = 256
TOKENS = 16384
CAP = 1


def draw_queries(key, part):
    sample = jax.random.truncated_normal(jax.random.fold_in(key, 1), -4.0, 4.0, (NBLK, BLOCK, QHEADS, HEAD), jnp.float32)
    return sample.reshape(TOKENS, QHEADS, HEAD).astype(jnp.bfloat16)


def draw_key_states(key, part):
    sample = jax.random.truncated_normal(jax.random.fold_in(key, 2), -4.0, 4.0, (NBLK, BLOCK, KV_HEADS, HEAD), jnp.float32)
    return sample.reshape(TOKENS, KV_HEADS, HEAD).astype(jnp.bfloat16)


def draw_selected(key, part):
    shard_count = NBLK // BLK_DEV
    group_count = QHEADS // QH_DEV
    request_count = BLK_DEV * QH_DEV * TOPK
    pop_key, score_key, block_key = jax.random.split(jax.random.fold_in(key, 3), 3)
    popularity = jax.random.randint(pop_key, (shard_count,), 0, 4)
    offsets = jnp.arange(shard_count - 1, dtype=jnp.int32)
    peers = (jnp.arange(shard_count, dtype=jnp.int32)[:, None] + 1 + offsets[None, :]) % shard_count
    random_score = jax.random.randint(score_key, (shard_count, group_count, shard_count - 1), 0, 8)
    weighted = (random_score + 3 * popularity[peers][:, None, :]) * shard_count + offsets[None, None, :]
    ranking = jnp.argsort(-weighted, axis=-1, stable=True)
    chosen = jnp.take_along_axis(jnp.broadcast_to(peers[:, None, :], weighted.shape), ranking, axis=-1)
    group_index = jnp.arange(request_count, dtype=jnp.int32) // CAP
    peer_shard = chosen[:, :, group_index]
    local_block = jax.random.randint(block_key, (shard_count, group_count, request_count), 0, BLK_DEV)
    block_id = peer_shard * BLK_DEV + local_block
    arranged = block_id.reshape(shard_count, group_count, TOPK, BLK_DEV, QH_DEV).transpose(0, 3, 1, 4, 2)
    return arranged.reshape(NBLK, QHEADS, TOPK).astype(jnp.int32)


def levels(key, shape, pieces, smallest, largest):
    level = 1.0
    for position, blocks in pieces:
        steps = jax.random.uniform(jax.random.fold_in(jax.random.fold_in(key, 6), position), (blocks,), jnp.float32, smallest / len(pieces), largest / len(pieces))
        level = level * jnp.repeat(jnp.exp(steps), shape[position] // blocks).reshape((-1,) + (1,) * (len(shape) - 1 - position))
    return level


def normal_values(stream_key, extent, deviation, bound, shards=(), kind=jnp.bfloat16):
    values = jax.random.normal(stream_key, extent, jnp.float32) * deviation
    if len(shards) > 0:
        values = levels(stream_key, extent, shards, -0.22, 0.18) * values
    return jnp.clip(values, min=-bound, max=bound).astype(kind)


def setup_inputs(seed: int = 0) -> dict:
    streams_of = jax.random.split(jax.random.key(seed), 6)
    queries = draw_queries(jax.random.fold_in(streams_of[5], 71), 0)
    key_states = draw_key_states(jax.random.fold_in(streams_of[5], 71), 0)
    value_states = normal_values(streams_of[2], (TOKENS, KV_HEADS, HEAD), 1.0, 5.0, ((0, 128),))
    grad_out = normal_values(streams_of[3], (TOKENS, QHEADS, HEAD), 1.0, 5.0, ((0, 128), (1, 4)))
    selected = draw_selected(jax.random.fold_in(streams_of[5], 71), 0)
    return {"queries": queries, "key_states": key_states, "value_states": value_states, "grad_out": grad_out, "selected": selected}


def rounded(values_in):
    return lax.optimization_barrier(values_in.astype(jnp.bfloat16)).astype(jnp.float32)


def reference(queries, key_states, value_states, grad_out, selected):
    total_rows, query_heads, head_size = queries.shape
    kv_heads = key_states.shape[1]
    blocks = total_rows // BLOCK
    factor = head_size ** -0.5
    query_blocks = queries.reshape(blocks, BLOCK, query_heads, head_size)
    grad_blocks = grad_out.reshape(blocks, BLOCK, query_heads, head_size)
    key_blocks = key_states.reshape(blocks, BLOCK, kv_heads, head_size)
    value_blocks = value_states.reshape(blocks, BLOCK, kv_heads, head_size)
    own_index = jnp.arange(blocks, dtype=jnp.int32)[:, None]

    def one_head(totals, head_index):
        key_acc, value_acc = totals
        kv_index = head_index % kv_heads
        query_now = lax.dynamic_index_in_dim(query_blocks, head_index, 2, keepdims=False).astype(jnp.float32)
        grad_now = lax.dynamic_index_in_dim(grad_blocks, head_index, 2, keepdims=False).astype(jnp.float32)
        key_head = lax.dynamic_index_in_dim(key_blocks, kv_index, 2, keepdims=False)
        value_head = lax.dynamic_index_in_dim(value_blocks, kv_index, 2, keepdims=False)
        routed = lax.dynamic_index_in_dim(selected, head_index, 1, keepdims=False).astype(jnp.int32)
        listed = jnp.concatenate([own_index, routed], axis=1)
        key_sel = key_head[listed].astype(jnp.float32)
        value_sel = value_head[listed].astype(jnp.float32)
        scores = jnp.einsum("nqh,ntkh->ntqk", query_now, key_sel) * factor
        block_max = jnp.max(scores, axis=-1)
        exp_scores = jnp.exp(scores - block_max[..., None])
        block_sum = jnp.sum(exp_scores, axis=-1)
        block_out = rounded(jnp.einsum("ntqk,ntkh->ntqh", rounded(exp_scores), value_sel))
        overall_max = jnp.max(block_max, axis=1)
        weight = jnp.exp(block_max - overall_max[:, None])
        denominator = jnp.sum(weight * block_sum, axis=1)
        attended = (jnp.sum(weight[..., None] * block_out, axis=1) / denominator[..., None]).astype(jnp.bfloat16)
        log_total = overall_max + jnp.log(denominator)
        row_delta = jnp.sum(grad_now * attended.astype(jnp.float32), axis=-1)
        probability = jnp.exp(scores - log_total[:, None, :, None])
        grad_prob = jnp.einsum("nqh,ntkh->ntqk", grad_now, value_sel)
        grad_scores = rounded(probability * (grad_prob - row_delta[:, None, :, None]))
        query_terms = rounded(jnp.einsum("ntqk,ntkh->ntqh", grad_scores, key_sel) * factor)
        query_total = jnp.sum(query_terms, axis=1).astype(jnp.bfloat16)
        key_terms = rounded(jnp.einsum("ntqk,nqh->ntkh", grad_scores, query_now) * factor)
        value_terms = rounded(jnp.einsum("ntqk,nqh->ntkh", rounded(probability), grad_now))
        key_head_sum = jnp.zeros((blocks, BLOCK, head_size), jnp.float32).at[listed].add(key_terms)
        value_head_sum = jnp.zeros((blocks, BLOCK, head_size), jnp.float32).at[listed].add(value_terms)
        key_acc = key_acc.at[kv_index].add(key_head_sum)
        value_acc = value_acc.at[kv_index].add(value_head_sum)
        return (key_acc, value_acc), (attended, query_total)

    start = jnp.zeros((kv_heads, blocks, BLOCK, head_size), jnp.float32)
    (key_acc, value_acc), (attended_all, query_all) = lax.scan(one_head, (start, start), jnp.arange(query_heads, dtype=jnp.int32))
    attention_out = attended_all.transpose(1, 2, 0, 3).reshape(total_rows, query_heads, head_size)
    query_grad = query_all.transpose(1, 2, 0, 3).reshape(total_rows, query_heads, head_size)
    key_grad = key_acc.transpose(1, 2, 0, 3).reshape(total_rows, kv_heads, head_size).astype(jnp.bfloat16)
    value_grad = value_acc.transpose(1, 2, 0, 3).reshape(total_rows, kv_heads, head_size).astype(jnp.bfloat16)
    return (attention_out, query_grad, key_grad, value_grad)
```

```python
import functools

import jax
import jax.numpy as jnp
from jax import lax
from jax.experimental import pallas as pl
from jax.experimental.pallas import tpu as pltpu
from jax.sharding import PartitionSpec as P

BLOCK = 64
HEAD = 128
SIDE = 4
PLANE = SIDE * SIDE
MESH = pl.DeviceIdType.MESH
ANY = pl.BlockSpec(memory_space=pl.ANY)
VMEM = pl.BlockSpec(memory_space=pltpu.VMEM)
SMEM = pl.BlockSpec(memory_space=pltpu.SMEM)


def place():
    ctx = lax.axis_index("ctx")
    x = lax.axis_index("head")
    return x, (ctx // 2) % SIDE, ctx // (2 * SIDE), ctx % 2


def ctx_of(z, y, core):
    return (z * SIDE + y) * 2 + core


def unit_of(x, y):
    return (y % 2) * 8 + 2 * x + y // 2


def greet(planes, x, y, z, core):
    barrier = pltpu.get_barrier_semaphore()

    def one(k, carry):
        t = (x * SIDE + y + k) % PLANE
        pl.semaphore_signal(
            barrier, inc=1, device_id=(ctx_of(z, t % SIDE, core), t // SIDE), device_id_type=MESH
        )
        return carry

    for other in (
        ctx_of((z + 1) % planes, y, core),
        ctx_of((z + planes - 1) % planes, y, core),
        ctx_of(z, y, 1 - core),
    ):
        pl.semaphore_signal(barrier, inc=1, device_id=(other, x), device_id_type=MESH)
    lax.fori_loop(1, PLANE, one, 0)
    pl.semaphore_wait(barrier, PLANE + 2)


def remote(src, dst, send, recv, ctx, x):
    return pltpu.make_async_remote_copy(
        src_ref=src, dst_ref=dst, send_sem=send, recv_sem=recv, device_id=(ctx, x), device_id_type=MESH
    )


def bring(
    planes,
    qd,
    sel,
    kv,
    qd_out,
    sel_out,
    store,
    near_send,
    near_recv,
    q_send,
    q_recv,
    i_send,
    i_recv,
    ring_send,
    ring_recv,
    pair_send,
    pair_recv,
    own_sem,
):
    x, y, z, core = place()
    half_way = planes // 2
    greet(planes, x, y, z, core)

    def near(d):
        to = (y + d) % SIDE
        return remote(
            kv.at[to // 2],
            store.at[pl.ds(z * 16 + core * 8 + y * 2, 2)],
            near_send.at[d - 1],
            near_recv.at[d - 1],
            ctx_of(z, to, core),
            x,
        )

    def query(k):
        t = (x * SIDE + y + k) % PLANE
        return remote(
            qd.at[unit_of(t // SIDE, t % SIDE)],
            qd_out.at[x * SIDE + y],
            q_send.at[k - 1],
            q_recv.at[k - 1],
            ctx_of(z, t % SIDE, core),
            t // SIDE,
        )

    def index(k):
        t = (x * SIDE + y + k) % PLANE
        return remote(
            sel.at[unit_of(t // SIDE, t % SIDE)],
            sel_out.at[x * SIDE + y],
            i_send.at[k - 1],
            i_recv.at[k - 1],
            ctx_of(z, t % SIDE, core),
            t // SIDE,
        )

    def rows(origin, half):
        return store.at[pl.ds(((origin + planes) % planes) * 16 + core * 8 + half * 4, 4)]

    def origin_of(d, s):
        return z - s if d == 0 else z + s

    def hop(d, s, half):
        to = (z + 1) % planes if d == 0 else (z + planes - 1) % planes
        piece = rows(origin_of(d, s - 1), half)
        return remote(
            piece,
            piece,
            ring_send.at[d, s - 1, half],
            ring_recv.at[d, s - 1, half],
            ctx_of(to, y, core),
            x,
        )

    def arrived(d, s, half):
        piece = rows(origin_of(d, s), half)
        return remote(
            piece,
            piece,
            ring_send.at[d, s - 1, half],
            ring_recv.at[d, s - 1, half],
            ctx_of(z, y, 1 - core),
            x,
        )

    def share(d, s, half):
        piece = rows(origin_of(d, s), half)
        return remote(
            piece,
            piece,
            pair_send.at[d, s, half],
            pair_recv.at[d, s, half],
            ctx_of(z, y, 1 - core),
            x,
        )

    def shared(d, s, half):
        piece = store.at[
            pl.ds(((origin_of(d, s) + planes) % planes) * 16 + (1 - core) * 8 + half * 4, 4)
        ]
        return remote(
            piece,
            piece,
            pair_send.at[d, s, half],
            pair_recv.at[d, s, half],
            ctx_of(z, y, 1 - core),
            x,
        )

    for d in range(1, SIDE):
        near(d).start()
    mine = (
        pltpu.make_async_copy(
            kv.at[y // 2], store.at[pl.ds(z * 16 + core * 8 + y * 2, 2)], own_sem.at[0]
        ),
        pltpu.make_async_copy(qd.at[unit_of(x, y)], qd_out.at[x * SIDE + y], own_sem.at[1]),
        pltpu.make_async_copy(sel.at[unit_of(x, y)], sel_out.at[x * SIDE + y], own_sem.at[2]),
    )
    for copy in mine:
        copy.start()

    def send_query(k, carry):
        query(k).start()
        index(k).start()
        return carry

    lax.fori_loop(1, PLANE, send_query, 0)
    mine[0].wait()
    for d in range(1, SIDE):
        near(d).wait_recv()

    for half in range(2):
        for d in range(2):
            hop(d, 1, half).start()
        share(0, 0, half).start()

    def step(s, carry):
        for half in range(2):
            for d in range(2):
                arrived(d, s - 1, half).wait_recv()
                hop(d, s, half).start()
                share(d, s - 1, half).start()
        return carry

    lax.fori_loop(2, half_way, step, 0)
    for half in range(2):
        for d in range(2):
            arrived(d, half_way - 1, half).wait_recv()
            if half == d:
                hop(d, half_way, half).start()
            share(d, half_way - 1, half).start()
    for d in range(2):
        arrived(d, half_way, d).wait_recv()
        share(d, half_way, d).start()

    for half in range(2):
        shared(0, 0, half).wait_recv()
        share(0, 0, half).wait_send()

    def finish(s, carry):
        for half in range(2):
            for d in range(2):
                hop(d, s, half).wait_send()
                shared(d, s, half).wait_recv()
                share(d, s, half).wait_send()
        return carry

    lax.fori_loop(1, half_way, finish, 0)
    for d in range(2):
        hop(d, half_way, d).wait_send()
        shared(d, half_way, d).wait_recv()
        share(d, half_way, d).wait_send()
        mine[d + 1].wait()
    for d in range(1, SIDE):
        near(d).wait_send()

    def finish_query(k, carry):
        query(k).wait()
        index(k).wait()
        return carry

    lax.fori_loop(1, PLANE, finish_query, 0)


def attend(sel, qd, store, od, acc_out, kv, acc, stage, load_sem, out_sem):
    x, y, z, core = place()
    parity = y % 2
    factor = HEAD**-0.5
    f32 = jnp.float32

    def row_of(u, t):
        if t == 0:
            return z * 16 + core * 8 + (u % SIDE) * 2 + parity
        n = sel[u, 0, t - 1]
        return (n // 16) * 16 + ((n // 2) % 2) * 8 + ((n // 4) % SIDE) * 2 + n % 2

    def fetch(u, carry):
        for t in range(4):
            pltpu.make_async_copy(store.at[row_of(u, t)], kv.at[u, t], load_sem.at[u]).start()
        return carry

    lax.fori_loop(0, PLANE, fetch, 0)

    def clear(i, carry):
        acc[pl.ds(i * 2, 2)] = jnp.zeros((2, 2, BLOCK, HEAD), f32)
        return carry

    lax.fori_loop(0, acc.shape[0] // 2, clear, 0)

    def one(u, carry):
        pltpu.make_async_copy(store.at[pl.ds(0, 4)], kv.at[u], load_sem.at[u]).wait()
        q = qd[u, 0]
        g = qd[u, 1]
        keys = kv[u, :, 0].reshape(4 * BLOCK, HEAD)
        values = kv[u, :, 1].reshape(4 * BLOCK, HEAD)
        nt = (((1,), (1,)), ((), ()))
        nn = (((1,), (0,)), ((), ()))
        tn = (((0,), (0,)), ((), ()))
        scores = lax.dot_general(q, keys, nt, preferred_element_type=f32) * factor
        top = jnp.max(scores, axis=1, keepdims=True)
        e = jnp.exp(scores - top)
        inverse = 1.0 / jnp.sum(e, axis=1, keepdims=True)
        prob = e * inverse
        prob_b = prob.astype(jnp.bfloat16)
        out = lax.dot_general(prob_b, values, nn, preferred_element_type=f32).astype(jnp.bfloat16)
        od[u, 0] = out
        delta = jnp.sum(g.astype(f32) * out.astype(f32), axis=1, keepdims=True)
        grad_prob = lax.dot_general(g, values, nt, preferred_element_type=f32)
        grad_scores = (prob * (grad_prob - delta)).astype(jnp.bfloat16)
        od[u, 1] = (
            lax.dot_general(grad_scores, keys, nn, preferred_element_type=f32) * factor
        ).astype(jnp.bfloat16)
        key_terms = lax.dot_general(grad_scores, q, tn, preferred_element_type=f32) * factor
        value_terms = lax.dot_general(prob_b, g, tn, preferred_element_type=f32)
        for t in range(4):
            row = row_of(u, t)
            part = slice(t * BLOCK, (t + 1) * BLOCK)
            acc[row, 0] += key_terms[part]
            acc[row, 1] += value_terms[part]
        return carry

    lax.fori_loop(0, PLANE, one, 0)

    pieces = stage.shape[0] // 16

    def leave(i):
        return pltpu.make_async_copy(
            stage.at[pl.ds(i * 16, 16)], acc_out.at[pl.ds(i * 16, 16)], out_sem.at[i]
        )

    def pack(i, carry):
        def four(k, c):
            at = pl.ds(i * 16 + k * 2, 2)
            stage[at] = acc[at].astype(jnp.bfloat16)
            return c

        lax.fori_loop(0, 8, four, 0)
        leave(i).start()
        return carry

    lax.fori_loop(0, pieces, pack, 0)

    def wait(i, carry):
        leave(i).wait()
        return carry

    lax.fori_loop(0, pieces, wait, 0)


def give(
    planes,
    od,
    acc,
    od_out,
    kvg,
    own,
    part,
    inbox,
    outbox,
    fin,
    spread,
    q_send,
    q_recv,
    pair_send,
    pair_recv,
    own_sem,
    ring_send,
    ring_recv,
    near_send,
    near_recv,
    mine_sem,
):
    x, y, z, core = place()
    half_way = planes // 2
    f32 = jnp.float32
    greet(planes, x, y, z, core)

    def chunk(d, s):
        far = half_way - s
        return (z + far) % planes if d == 0 else (z + planes - far) % planes

    def pair(at):
        return remote(
            acc.at[pl.ds(at * 16 + (1 - core) * 8, 8)],
            part.at[at],
            pair_send.at[at],
            pair_recv.at[at],
            ctx_of(z, y, 1 - core),
            x,
        )

    def load(at):
        return pltpu.make_async_copy(
            acc.at[pl.ds(at * 16 + core * 8, 8)], own.at[at], own_sem.at[at]
        )

    def hop(d, s, half):
        to = (z + 1) % planes if d == 0 else (z + planes - 1) % planes
        return remote(
            outbox.at[d, s, half],
            inbox.at[d, s, half],
            ring_send.at[d, s, half],
            ring_recv.at[d, s, half],
            ctx_of(to, y, core),
            x,
        )

    def answer(k):
        t = (x * SIDE + y + k) % PLANE
        return remote(
            od.at[t],
            od_out.at[unit_of(x, y)],
            q_send.at[k - 1],
            q_recv.at[k - 1],
            ctx_of(z, t % SIDE, core),
            t // SIDE,
        )

    def near(d):
        to = (y + d) % SIDE
        return remote(
            fin.at[pl.ds(to * 2, 2)],
            spread.at[y],
            near_send.at[d - 1],
            near_recv.at[d - 1],
            ctx_of(z, to, core),
            x,
        )

    def begin(at):
        pair(at).start()
        load(at).start()

    def ready(at):
        load(at).wait()
        pair(at).wait_recv()

    def here(at, half):
        span = pl.ds(half * 4, 4)
        return own[at, span].astype(f32) + part[at, span].astype(f32)

    def emit(d, s, half, extra):
        total = here(chunk(d, s), half)
        if extra:
            hop(d, s - 1, half).wait_recv()
            total += inbox[d, s - 1, half].astype(f32)
        outbox[d, s, half] = total.astype(jnp.bfloat16)
        hop(d, s, half).start()

    begin(chunk(0, 0))

    def begin_step(s, carry):
        begin(chunk(0, s))
        begin(chunk(1, s))
        return carry

    lax.fori_loop(1, half_way, begin_step, 0)
    begin(z)

    home = pltpu.make_async_copy(od.at[x * SIDE + y], od_out.at[unit_of(x, y)], mine_sem)
    home.start()

    def send_answer(k, carry):
        answer(k).start()
        return carry

    lax.fori_loop(1, PLANE, send_answer, 0)

    ready(chunk(0, 0))
    for d in range(2):
        emit(d, 0, d, False)
    for d in range(2):
        ready(chunk(d, 1))
        for half in range(2):
            emit(d, 1, half, half == d)

    def step(s, carry):
        for d in range(2):
            ready(chunk(d, s))
        for half in range(2):
            for d in range(2):
                emit(d, s, half, True)
        return carry

    lax.fori_loop(2, half_way, step, 0)
    ready(z)
    for half in range(2):
        total = here(z, half)
        for d in range(2):
            hop(d, half_way - 1, half).wait_recv()
            total += inbox[d, half_way - 1, half].astype(f32)
        fin[pl.ds(half * 4, 4)] = total.astype(jnp.bfloat16)
    for d in range(1, SIDE):
        near(d).start()
    spread[y] = fin[pl.ds(y * 2, 2)]

    def finish(s, carry):
        for d in range(2):
            for half in range(2):
                hop(d, s, half).wait_send()
        return carry

    lax.fori_loop(1, half_way, finish, 0)
    for d in range(2):
        hop(d, 0, d).wait_send()

    def finish_pair(at, carry):
        pair(at).wait_send()
        return carry

    lax.fori_loop(0, planes, finish_pair, 0)

    def finish_answer(k, carry):
        answer(k).wait()
        return carry

    lax.fori_loop(1, PLANE, finish_answer, 0)
    home.wait()
    for d in range(1, SIDE):
        near(d).wait()
    for pick in range(2):
        kvg[pick] = (spread[2 * pick].astype(f32) + spread[2 * pick + 1].astype(f32)).astype(
            jnp.bfloat16
        )


def local(planes, queries, key_states, value_states, grad_out, selected):
    bf16 = jnp.bfloat16
    dma = pltpu.SemaphoreType.DMA
    half_way = planes // 2
    x = lax.axis_index("head")
    ctx = lax.axis_index("ctx")
    heads = queries.shape[1]

    qd = (
        jnp.stack([queries, grad_out])
        .reshape(2, 2, BLOCK, heads, HEAD)
        .transpose(1, 3, 0, 2, 4)
        .reshape(PLANE, 2, BLOCK, HEAD)
    )
    kv = (
        lax.dynamic_slice_in_dim(jnp.stack([key_states, value_states]), 2 * x, 2, 2)
        .reshape(2, 2, BLOCK, 2, HEAD)
        .transpose(3, 1, 0, 2, 4)
    )
    sel = lax.dynamic_slice_in_dim(selected, 2 * ctx, 2, 0).reshape(PLANE, 1, 3)
    sel = jnp.pad(sel, ((0, 0), (0, 0), (0, HEAD - 3)))

    shape = jax.ShapeDtypeStruct
    units = shape((PLANE, 2, BLOCK, HEAD), bf16)
    rows = shape((planes * 16, 2, BLOCK, HEAD), bf16)

    qd_all, sel_all, store = pl.pallas_call(
        functools.partial(bring, planes),
        name="bring",
        out_shape=(units, shape((PLANE, 1, HEAD), jnp.int32), rows),
        in_specs=[VMEM, VMEM, VMEM],
        out_specs=(ANY, ANY, ANY),
        scratch_shapes=[
            dma((SIDE - 1,)),
            dma((SIDE - 1,)),
            dma((PLANE - 1,)),
            dma((PLANE - 1,)),
            dma((PLANE - 1,)),
            dma((PLANE - 1,)),
            dma((2, half_way, 2)),
            dma((2, half_way, 2)),
            dma((2, half_way + 1, 2)),
            dma((2, half_way + 1, 2)),
            dma((3,)),
        ],
        compiler_params=pltpu.CompilerParams(collective_id=0, has_side_effects=True),
    )(qd, sel, kv)

    od, acc = pl.pallas_call(
        attend,
        name="attend",
        out_shape=(units, rows),
        in_specs=[SMEM, VMEM, ANY],
        out_specs=(VMEM, ANY),
        scratch_shapes=[
            pltpu.VMEM((PLANE, 4, 2, BLOCK, HEAD), bf16),
            pltpu.VMEM((planes * 16, 2, BLOCK, HEAD), jnp.float32),
            pltpu.VMEM((planes * 16, 2, BLOCK, HEAD), bf16),
            dma((PLANE,)),
            dma((planes,)),
        ],
        compiler_params=pltpu.CompilerParams(vmem_limit_bytes=48 * 1024 * 1024),
    )(sel_all, qd_all, store)

    piece = (4, 2, BLOCK, HEAD)
    od_all, kvg = pl.pallas_call(
        functools.partial(give, planes),
        name="give",
        out_shape=(units, shape((2, 2, 2, BLOCK, HEAD), bf16)),
        in_specs=[VMEM, ANY],
        out_specs=(ANY, VMEM),
        scratch_shapes=[
            pltpu.VMEM((planes, 8, 2, BLOCK, HEAD), bf16),
            pltpu.VMEM((planes, 8, 2, BLOCK, HEAD), bf16),
            pltpu.VMEM((2, half_way, 2, *piece), bf16),
            pltpu.VMEM((2, half_way, 2, *piece), bf16),
            pltpu.VMEM((8, 2, BLOCK, HEAD), bf16),
            pltpu.VMEM((SIDE, 2, 2, BLOCK, HEAD), bf16),
            dma((PLANE - 1,)),
            dma((PLANE - 1,)),
            dma((planes,)),
            dma((planes,)),
            dma((planes,)),
            dma((2, half_way, 2)),
            dma((2, half_way, 2)),
            dma((SIDE - 1,)),
            dma((SIDE - 1,)),
            dma,
        ],
        compiler_params=pltpu.CompilerParams(
            collective_id=1, has_side_effects=True, vmem_limit_bytes=32 * 1024 * 1024
        ),
    )(od, acc)

    od_all = (
        od_all.reshape(2, heads, 2, BLOCK, HEAD)
        .transpose(2, 0, 3, 1, 4)
        .reshape(2, 2 * BLOCK, heads, HEAD)
    )
    kvg = kvg.transpose(2, 1, 3, 0, 4).reshape(2, 2 * BLOCK, 2, HEAD)
    return od_all[0], od_all[1], kvg[0], kvg[1]


def solution(mesh):
    planes = mesh.shape["ctx"] // (2 * SIDE)
    spread = P("ctx", "head", None)
    whole = P("ctx", None, None)
    return jax.shard_map(
        functools.partial(local, planes),
        mesh=mesh,
        in_specs=(spread, whole, whole, spread, P(None, "head", None)),
        out_specs=(spread, spread, spread, spread),
        check_vma=False,
    )
```

```python
import functools

import jax
import jax.numpy as jnp
from jax import lax
from jax.experimental import pallas as pl
from jax.experimental.pallas import tpu as pltpu
from jax.sharding import PartitionSpec as P

BLOCK = 64
HEAD = 128
SIDE = 4
PLANE = SIDE * SIDE
MESH = pl.DeviceIdType.MESH
VMEM = pl.BlockSpec(memory_space=pltpu.VMEM)
SMEM = pl.BlockSpec(memory_space=pltpu.SMEM)
HBM = pl.BlockSpec(memory_space=pltpu.HBM)

HALVES = ((0, 1), (2, 1))


def place():
    ctx = lax.axis_index("ctx")
    x = lax.axis_index("head")
    return x, (ctx // 2) % SIDE, ctx // (2 * SIDE), ctx % 2


def ctx_of(z, y, core):
    return (z * SIDE + y) * 2 + core


def unit_of(x, y):
    return (y % 2) * 8 + 2 * x + y // 2


def piece_of(parity, i):
    return (3 * parity, parity + 1, 2 - parity)[i]


def greet(planes, x, y, z, core):
    barrier = pltpu.get_barrier_semaphore()

    def one(k, carry):
        t = (x * SIDE + y + k) % PLANE
        pl.semaphore_signal(
            barrier, inc=1, device_id=(ctx_of(z, t % SIDE, core), t // SIDE), device_id_type=MESH
        )
        return carry

    for other in (
        ctx_of((z + 1) % planes, y, core),
        ctx_of((z + planes - 1) % planes, y, core),
        ctx_of(z, y, 1 - core),
        ctx_of(z, y + 1 - 2 * (y % 2), 1 - core),
    ):
        pl.semaphore_signal(barrier, inc=1, device_id=(other, x), device_id_type=MESH)
    lax.fori_loop(1, PLANE, one, 0)
    pl.semaphore_wait(barrier, PLANE + 3)


def remote(src, dst, send, recv, ctx, x):
    return pltpu.make_async_remote_copy(
        src_ref=src, dst_ref=dst, send_sem=send, recv_sem=recv, device_id=(ctx, x), device_id_type=MESH
    )


def bring(
    planes,
    q_hbm,
    g_hbm,
    k_hbm,
    v_hbm,
    sel_hbm,
    qd_out,
    sel_out,
    store,
    q,
    g,
    k,
    v,
    sel,
    qd,
    kv,
    sel_all,
    load_sem,
    near_send,
    near_recv,
    q_send,
    q_recv,
    i_send,
    i_recv,
    ring_send,
    ring_recv,
    pair_send,
    pair_recv,
    mate_send,
    mate_recv,
    over_send,
    over_recv,
    own_sem,
):
    x, y, z, core = place()
    half_way = planes // 2
    last = half_way - 1
    parity = y % 2
    mate = y + 1 - 2 * parity
    heads = q.shape[1]

    loads = [
        pltpu.make_async_copy(src, dst, load_sem.at[i])
        for i, (src, dst) in enumerate(
            ((k_hbm, k), (v_hbm, v), (q_hbm, q), (g_hbm, g), (sel_hbm, sel))
        )
    ]
    for copy in loads:
        copy.start()
    for copy in loads[:2]:
        copy.wait()
    for b in range(2):
        tokens = pl.ds(b * BLOCK, BLOCK)
        kv[:, b, 0] = jnp.swapaxes(k[tokens], 0, 1)
        kv[:, b, 1] = jnp.swapaxes(v[tokens], 0, 1)
    greet(planes, x, y, z, core)

    def near(d):
        to = (y + d) % SIDE
        return remote(
            kv.at[2 * x + to // 2],
            store.at[pl.ds(z * 16 + core * 8 + y * 2, 2)],
            near_send.at[d - 1],
            near_recv.at[d - 1],
            ctx_of(z, to, core),
            x,
        )

    def query(i):
        t = (x * SIDE + y + i) % PLANE
        return remote(
            qd.at[unit_of(t // SIDE, t % SIDE)],
            qd_out.at[x * SIDE + y],
            q_send.at[i - 1],
            q_recv.at[i - 1],
            ctx_of(z, t % SIDE, core),
            t // SIDE,
        )

    def index(d):
        return remote(
            sel, sel_all.at[x], i_send.at[d - 1], i_recv.at[d - 1], ctx_of(z, y, core), (x + d) % SIDE
        )

    def at(d, j, side, first, count):
        origin = (z + planes - j) % planes if d == 0 else (z + j) % planes
        return store.at[pl.ds(origin * 16 + side * 8 + first, count)]

    def piece(d, j, side, i, split):
        first = 2 * piece_of(parity, i)
        if split and i == 1:
            return at(d, j, side, first + d, 1)
        return at(d, j, side, first, 2)

    def hop(d, s, i, split=False):
        to = (z + 1) % planes if d == 0 else (z + planes - 1) % planes
        part = piece(d, s - 1, core, i, split)
        sems = ring_send.at[d, s - 1, i], ring_recv.at[d, s - 1, i]
        return remote(part, part, *sems, ctx_of(to, y, core), x)

    def arrived(d, s, i, split=False):
        part = piece(d, s, core, i, split)
        sems = ring_send.at[d, s - 1, i], ring_recv.at[d, s - 1, i]
        return remote(part, part, *sems, ctx_of(z, y, 1 - core), x)

    def share(d, s, i, side, split=False):
        part = piece(d, s, side, i, split)
        sems = pair_send.at[d, s - 1, i], pair_recv.at[d, s - 1, i]
        return remote(part, part, *sems, ctx_of(z, y, 1 - core), x)

    def share_own(side):
        part = at(0, 0, side, 0, 8)
        sems = own_sem.at[1], own_sem.at[2]
        return remote(part, part, *sems, ctx_of(z, y, 1 - core), x)

    def cross(d, s, first):
        part = at(d, s, core, 6 * first, 2)
        sems = mate_send.at[d, s - 1], mate_recv.at[d, s - 1]
        return remote(part, part, *sems, ctx_of(z, mate, core), x)

    def over(d, s, side):
        part = at(d, s, side, 6 * (1 - parity), 2)
        sems = over_send.at[d, s - 1], over_recv.at[d, s - 1]
        return remote(part, part, *sems, ctx_of(z, y, 1 - core), x)

    def cross_over(first, side):
        part = at(0, half_way, side, 6 * first, 2)
        sems = over_send.at[0, last], over_recv.at[0, last]
        return remote(part, part, *sems, ctx_of(z, mate, 1 - core), x)

    for d in range(1, SIDE):
        near(d).start()
    mine = pltpu.make_async_copy(
        kv.at[2 * x + y // 2], store.at[pl.ds(z * 16 + core * 8 + y * 2, 2)], own_sem.at[0]
    )
    mine.start()
    for copy in loads[2:]:
        copy.wait()
    for d in range(1, SIDE):
        index(d).start()
    for b in range(2):
        tokens = pl.ds(b * BLOCK, BLOCK)
        units = pl.ds(b * heads, heads)
        qd[units, 0] = jnp.swapaxes(q[tokens], 0, 1)
        qd[units, 1] = jnp.swapaxes(g[tokens], 0, 1)
    mine.wait()
    for d in range(1, SIDE):
        near(d).wait_recv()
    for i in range(3):
        for d in range(2):
            hop(d, 1, i).start()
    share_own(core).start()

    def send_query(i, carry):
        query(i).start()
        return carry

    lax.fori_loop(1, PLANE, send_query, 0)
    qd_out[x * SIDE + y] = qd[unit_of(x, y)]
    sel_all[x] = sel[...]

    def step(s, carry):
        for i in range(3):
            for d in range(2):
                arrived(d, s - 1, i).wait_recv()
                hop(d, s, i).start()
                if i == 0:
                    cross(d, s - 1, parity).start()
                share(d, s - 1, i, core).start()

        @pl.when(s > 2)
        def _():
            for d in range(2):
                cross(d, s - 2, 1 - parity).wait_recv()
                over(d, s - 2, core).start()

        return carry

    lax.fori_loop(2, half_way, step, 0)
    for i in range(3):
        for d in range(2):
            arrived(d, last, i).wait_recv()
            if i in HALVES[d]:
                hop(d, half_way, i, True).start()
            if i == 0:
                cross(d, last, parity).start()
            share(d, last, i, core).start()
    for d in range(2):
        cross(d, last - 1, 1 - parity).wait_recv()
        over(d, last - 1, core).start()
    for k in range(2):
        for d in range(2):
            i = HALVES[d][k]
            arrived(d, half_way, i, True).wait_recv()
            if i == 0:
                cross(0, half_way, parity).start()
                cross_over(parity, core).start()
            share(d, half_way, i, core, True).start()
    for d in range(2):
        cross(d, last, 1 - parity).wait_recv()
        over(d, last, core).start()

    def finish_query(i, carry):
        query(i).wait()
        return carry

    lax.fori_loop(1, PLANE, finish_query, 0)
    for d in range(1, SIDE):
        index(d).wait()
    own_head = lax.broadcasted_iota(jnp.int32, sel.shape, 1) == 2 * x + y // 2
    for group in range(SIDE):
        sel_out[group] = jnp.sum(jnp.where(own_head, sel_all[group], 0), axis=1)

    for d in range(1, SIDE):
        near(d).wait_send()
    share_own(1 - core).wait_recv()
    share_own(core).wait_send()

    def finish(s, carry):
        for d in range(2):
            for i in range(3):
                hop(d, s, i).wait_send()
                share(d, s, i, 1 - core).wait_recv()
                share(d, s, i, core).wait_send()
            cross(d, s, parity).wait_send()
            over(d, s, 1 - core).wait_recv()
            over(d, s, core).wait_send()
        return carry

    lax.fori_loop(1, half_way, finish, 0)
    for d in range(2):
        for i in HALVES[d]:
            hop(d, half_way, i, True).wait_send()
            share(d, half_way, i, 1 - core, True).wait_recv()
            share(d, half_way, i, core, True).wait_send()
    cross(0, half_way, parity).wait_send()
    cross_over(parity, core).wait_send()
    cross(0, half_way, 1 - parity).wait_recv()
    cross_over(1 - parity, 1 - core).wait_recv()


def attend(sel, qd, store, od, acc):
    x, y, z, core = place()
    parity = y % 2
    factor = HEAD**-0.5
    f32, bf16 = jnp.float32, jnp.bfloat16
    nt = (((1,), (1,)), ((), ()))
    nn = (((1,), (0,)), ((), ()))
    tn = (((0,), (0,)), ((), ()))

    def clear(i, carry):
        acc[pl.ds(i * 4, 4)] = jnp.zeros((4, 2, BLOCK, HEAD), bf16)
        return carry

    lax.fori_loop(0, acc.shape[0] // 4, clear, 0)

    def dot(a, b, dims):
        return lax.dot_general(a, b, dims, preferred_element_type=f32)

    def one(side, carry):
        own = z * 16 + core * 8 + side * 2 + parity
        block = ((z * SIDE + side) * 2 + core) * 2 + parity
        own_terms = [jnp.zeros((BLOCK, HEAD), f32)] * 2
        for group in range(SIDE):
            u = group * SIDE + side
            rows = [own]
            for t in range(3):
                n = sel[group, t, block]
                rows.append((n // 16) * 16 + ((n // 2) % 2) * 8 + ((n // 4) % SIDE) * 2 + n % 2)
            q = qd[u, 0]
            g = qd[u, 1]
            keys = jnp.concatenate([store[r, 0] for r in rows], axis=0)
            values = jnp.concatenate([store[r, 1] for r in rows], axis=0)
            scores = dot(q, keys, nt) * factor
            top = jnp.max(scores, axis=1, keepdims=True)
            e = jnp.exp(scores - top)
            prob = e * (1.0 / jnp.sum(e, axis=1, keepdims=True))
            prob_b = prob.astype(bf16)
            out = dot(prob_b, values, nn).astype(bf16)
            od[u, 0] = out
            delta = jnp.sum(g.astype(f32) * out.astype(f32), axis=1, keepdims=True)
            grad_prob = dot(g, values, nt)
            grad_scores = (prob * (grad_prob - delta)).astype(bf16)
            od[u, 1] = (dot(grad_scores, keys, nn) * factor).astype(bf16)
            terms = dot(grad_scores, q, tn) * factor, dot(prob_b, g, tn)
            for i in range(2):
                own_terms[i] += terms[i][:BLOCK]
                for t in range(1, 4):
                    part = terms[i][t * BLOCK : (t + 1) * BLOCK]
                    acc[rows[t], i] = (acc[rows[t], i].astype(f32) + part).astype(bf16)
        for i in range(2):
            acc[own, i] = (acc[own, i].astype(f32) + own_terms[i]).astype(bf16)
        return carry

    lax.fori_loop(0, SIDE, one, 0)


def give(
    planes,
    od,
    acc,
    att,
    grad_q,
    kvg,
    part,
    inbox,
    outbox,
    mate_in,
    mate_out,
    fin,
    spread,
    od_all,
    q_send,
    q_recv,
    pair_send,
    pair_recv,
    mate_send,
    mate_recv,
    ring_send,
    ring_recv,
    near_send,
    near_recv,
    mine_sem,
):
    x, y, z, core = place()
    half_way = planes // 2
    parity = y % 2
    mate = y + 1 - 2 * parity
    heads = att.shape[1]
    f32, bf16 = jnp.float32, jnp.bfloat16

    for d in range(2):
        inbox[d, 0, 1, 1 - d] = jnp.zeros((2, BLOCK, HEAD), bf16)
    greet(planes, x, y, z, core)

    def chunk(d, s):
        far = half_way - s
        return (z + far) % planes if d == 0 else (z + planes - far) % planes

    def pair(at):
        return remote(
            acc.at[pl.ds(at * 16 + (1 - core) * 8, 8)],
            part.at[at],
            pair_send.at[at],
            pair_recv.at[at],
            ctx_of(z, y, 1 - core),
            x,
        )

    def cross(at):
        return remote(
            mate_out.at[at],
            mate_in.at[at],
            mate_send.at[at],
            mate_recv.at[at],
            ctx_of(z, mate, core),
            x,
        )

    def hop(d, s, i):
        to = (z + 1) % planes if d == 0 else (z + planes - 1) % planes
        box = (d, s, i, pl.ds(d, 1)) if isinstance(s, int) and s == 0 and i == 1 else (d, s, i)
        return remote(
            outbox.at[box],
            inbox.at[box],
            ring_send.at[d, s, i],
            ring_recv.at[d, s, i],
            ctx_of(to, y, core),
            x,
        )

    def answer(i):
        t = (x * SIDE + y + i) % PLANE
        return remote(
            od.at[t],
            od_all.at[unit_of(x, y)],
            q_send.at[i - 1],
            q_recv.at[i - 1],
            ctx_of(z, t % SIDE, core),
            t // SIDE,
        )

    def near(d):
        to = (y + d) % SIDE
        return remote(
            fin.at[pl.ds(to * 2, 2)],
            spread.at[y],
            near_send.at[d - 1],
            near_recv.at[d - 1],
            ctx_of(z, to, core),
            x,
        )

    def chip_sum(at, first, count):
        mine = acc[pl.ds(at * 16 + core * 8 + first, count)].astype(f32)
        return mine + part[at, pl.ds(first, count)].astype(f32)

    def prepare(at):
        pair(at).wait_recv()
        mate_out[at] = chip_sum(at, 6 * (1 - parity), 2).astype(bf16)
        cross(at).start()

    def emit(d, s, i, extra):
        at = chunk(d, s)
        total = chip_sum(at, 2 * piece_of(parity, i), 2)
        if i == 0:
            total += mate_in[at].astype(f32)
        if extra:
            hop(d, s - 1, i).wait_recv()
            total += inbox[d, s - 1, i].astype(f32)
        outbox[d, s, i] = total.astype(bf16)
        hop(d, s, i).start()

    pair(chunk(0, 0)).start()

    def begin_step(s, carry):
        pair(chunk(0, s)).start()
        pair(chunk(1, s)).start()
        return carry

    lax.fori_loop(1, half_way, begin_step, 0)
    pair(z).start()

    home = pltpu.make_async_copy(od.at[x * SIDE + y], od_all.at[unit_of(x, y)], mine_sem)
    home.start()

    def send_answer(i, carry):
        answer(i).start()
        return carry

    prepare(chunk(0, 0))
    for d in range(2):
        emit(d, 0, 1, False)
    emit(1, 0, 2, False)
    for d in range(2):
        prepare(chunk(d, 1))
    cross(chunk(0, 0)).wait_recv()
    emit(0, 0, 0, False)
    lax.fori_loop(1, PLANE, send_answer, 0)
    for d in range(2):
        prepare(chunk(d, 2))
    for i in (2, 1, 0):
        for d in range(2):
            if i == 0:
                cross(chunk(d, 1)).wait_recv()
            emit(d, 1, i, i in HALVES[d])

    def step(s, carry):
        @pl.when(s + 1 < half_way)
        def _():
            for d in range(2):
                prepare(chunk(d, s + 1))

        for i in (2, 1, 0):
            for d in range(2):
                if i == 0:
                    cross(chunk(d, s)).wait_recv()
                emit(d, s, i, True)
        return carry

    lax.fori_loop(2, half_way, step, 0)

    def finish_answer(i, carry):
        answer(i).wait()
        return carry

    lax.fori_loop(1, PLANE, finish_answer, 0)
    home.wait()
    for b in range(2):
        tokens = pl.ds(b * BLOCK, BLOCK)
        units = pl.ds(b * heads, heads)
        att[tokens] = jnp.swapaxes(od_all[units, 0], 0, 1)
        grad_q[tokens] = jnp.swapaxes(od_all[units, 1], 0, 1)

    pair(z).wait_recv()
    rest = 6 * (1 - parity)
    fin[pl.ds(rest, 2)] = chip_sum(z, rest, 2).astype(bf16)
    for i in (2, 1, 0):
        first = 2 * piece_of(parity, i)
        total = chip_sum(z, first, 2)
        for d in range(2):
            hop(d, half_way - 1, i).wait_recv()
            total += inbox[d, half_way - 1, i].astype(f32)
        fin[pl.ds(first, 2)] = total.astype(bf16)
    for d in range(1, SIDE):
        near(d).start()
    spread[y] = fin[pl.ds(y * 2, 2)]

    def finish(s, carry):
        for d in range(2):
            for i in range(3):
                hop(d, s, i).wait_send()
            cross(chunk(d, s)).wait_send()
            pair(chunk(d, s)).wait_send()
        return carry

    lax.fori_loop(1, half_way, finish, 0)
    for d in range(2):
        for i in HALVES[d]:
            hop(d, 0, i).wait_send()
    cross(chunk(0, 0)).wait_send()
    pair(chunk(0, 0)).wait_send()
    pair(z).wait_send()

    for d in range(1, SIDE):
        near(d).wait()
    for pick in range(2):
        kvg[pick] = (spread[2 * pick].astype(f32) + spread[2 * pick + 1].astype(f32)).astype(bf16)


def leave(att, grad_q, kvg, att_out, grad_q_out, grad_k_out, grad_v_out, pair, sem):
    copies = [
        pltpu.make_async_copy(src, dst, sem.at[i])
        for i, (src, dst) in enumerate(
            (
                (att, att_out),
                (grad_q, grad_q_out),
                (pair.at[0], grad_k_out),
                (pair.at[1], grad_v_out),
            )
        )
    ]
    for copy in copies[:2]:
        copy.start()
    for b in range(2):
        for i in range(2):
            pair[i, pl.ds(b * BLOCK, BLOCK)] = jnp.swapaxes(kvg[:, b, i], 0, 1)
    for copy in copies[2:]:
        copy.start()
    for copy in copies:
        copy.wait()


def local(planes, queries, key_states, value_states, grad_out, selected):
    bf16 = jnp.bfloat16
    dma = pltpu.SemaphoreType.DMA
    half_way = planes // 2
    heads = queries.shape[1]
    blocks = selected.shape[0]

    shape = jax.ShapeDtypeStruct
    units = (PLANE, 2, BLOCK, HEAD)
    rows = (planes * 16, 2, BLOCK, HEAD)
    lists = (3, heads, blocks)
    given = queries, grad_out, key_states, value_states, selected.transpose(2, 1, 0)

    qd, sel, store = pl.pallas_call(
        functools.partial(bring, planes),
        name="bring",
        out_shape=(shape(units, bf16), shape((SIDE, 3, blocks), jnp.int32), shape(rows, bf16)),
        in_specs=[HBM] * 5,
        out_specs=(VMEM,) * 3,
        scratch_shapes=[
            pltpu.VMEM(queries.shape, bf16),
            pltpu.VMEM(queries.shape, bf16),
            pltpu.VMEM(queries.shape, bf16),
            pltpu.VMEM(queries.shape, bf16),
            pltpu.VMEM(lists, jnp.int32),
            pltpu.VMEM(units, bf16),
            pltpu.VMEM((heads, 2, 2, BLOCK, HEAD), bf16),
            pltpu.VMEM((SIDE, *lists), jnp.int32),
            dma((5,)),
            dma((SIDE - 1,)),
            dma((SIDE - 1,)),
            dma((PLANE - 1,)),
            dma((PLANE - 1,)),
            dma((SIDE - 1,)),
            dma((SIDE - 1,)),
            dma((2, half_way, 3)),
            dma((2, half_way, 3)),
            dma((2, half_way, 3)),
            dma((2, half_way, 3)),
            dma((2, half_way)),
            dma((2, half_way)),
            dma((2, half_way)),
            dma((2, half_way)),
            dma((3,)),
        ],
        compiler_params=pltpu.CompilerParams(
            collective_id=0, has_side_effects=True, vmem_limit_bytes=16 * 1024 * 1024
        ),
    )(*(pltpu.with_memory_space_constraint(a, pltpu.HBM) for a in given))

    od, acc = pl.pallas_call(
        attend,
        name="attend",
        out_shape=(shape(units, bf16), shape(rows, bf16)),
        in_specs=[SMEM, VMEM, VMEM],
        out_specs=(VMEM, VMEM),
        compiler_params=pltpu.CompilerParams(vmem_limit_bytes=24 * 1024 * 1024),
    )(sel, qd, store)

    piece = (3, 2, 2, BLOCK, HEAD)
    att, grad_q, kvg = pl.pallas_call(
        functools.partial(give, planes),
        name="give",
        out_shape=(
            shape(queries.shape, bf16),
            shape(queries.shape, bf16),
            shape((2, 2, 2, BLOCK, HEAD), bf16),
        ),
        in_specs=[VMEM, VMEM],
        out_specs=(VMEM,) * 3,
        scratch_shapes=[
            pltpu.VMEM((planes, 8, 2, BLOCK, HEAD), bf16),
            pltpu.VMEM((2, half_way, *piece), bf16),
            pltpu.VMEM((2, half_way, *piece), bf16),
            pltpu.VMEM((planes, 2, 2, BLOCK, HEAD), bf16),
            pltpu.VMEM((planes, 2, 2, BLOCK, HEAD), bf16),
            pltpu.VMEM((8, 2, BLOCK, HEAD), bf16),
            pltpu.VMEM((SIDE, 2, 2, BLOCK, HEAD), bf16),
            pltpu.VMEM(units, bf16),
            dma((PLANE - 1,)),
            dma((PLANE - 1,)),
            dma((planes,)),
            dma((planes,)),
            dma((planes,)),
            dma((planes,)),
            dma((2, half_way, 3)),
            dma((2, half_way, 3)),
            dma((SIDE - 1,)),
            dma((SIDE - 1,)),
            dma,
        ],
        compiler_params=pltpu.CompilerParams(
            collective_id=1, has_side_effects=True, vmem_limit_bytes=28 * 1024 * 1024
        ),
    )(od, acc)

    key_shape = (2 * BLOCK, 2, HEAD)
    return pl.pallas_call(
        leave,
        name="leave",
        out_shape=(
            shape(queries.shape, bf16),
            shape(queries.shape, bf16),
            shape(key_shape, bf16),
            shape(key_shape, bf16),
        ),
        in_specs=[VMEM] * 3,
        out_specs=(HBM,) * 4,
        scratch_shapes=[pltpu.VMEM((2, *key_shape), bf16), dma((4,))],
        compiler_params=pltpu.CompilerParams(vmem_limit_bytes=4 * 1024 * 1024),
    )(att, grad_q, kvg)


def solution(mesh):
    planes = mesh.shape["ctx"] // (2 * SIDE)
    spread = P("ctx", "head", None)
    whole = P("ctx", None, None)
    return jax.shard_map(
        functools.partial(local, planes),
        mesh=mesh,
        in_specs=(spread, whole, whole, spread, P(None, "head", None)),
        out_specs=(spread, spread, spread, spread),
        check_vma=False,
    )
```

```python
import functools
import math

import jax
import jax.numpy as jnp
from jax import lax
from jax.experimental import pallas as pl
from jax.experimental.pallas import tpu as pltpu
from jax.sharding import PartitionSpec as P

BLOCK = 64
HEAD = 128
SIDE = 4
PLANE = SIDE * SIDE
MESH = pl.DeviceIdType.MESH
VMEM = pl.BlockSpec(memory_space=pltpu.VMEM)
SMEM = pl.BlockSpec(memory_space=pltpu.SMEM)
HBM = pl.BlockSpec(memory_space=pltpu.HBM)

HALVES = ((0, 1), (2, 1))


def place():
    ctx = lax.axis_index("ctx")
    x = lax.axis_index("head")
    return x, (ctx // 2) % SIDE, ctx // (2 * SIDE), ctx % 2


def ctx_of(z, y, core):
    return (z * SIDE + y) * 2 + core


def unit_of(x, y):
    return (y % 2) * 8 + 2 * x + y // 2


def piece_of(parity, i):
    return (3 * parity, parity + 1, 2 - parity)[i]


def announce(planes, x, y, z, core):
    barrier = pltpu.get_barrier_semaphore()

    def one(k, carry):
        t = (x * SIDE + y + k) % PLANE
        pl.semaphore_signal(
            barrier, inc=1, device_id=(ctx_of(z, t % SIDE, core), t // SIDE), device_id_type=MESH
        )
        return carry

    for other in (
        ctx_of((z + 1) % planes, y, core),
        ctx_of((z + planes - 1) % planes, y, core),
        ctx_of((z + planes + 1 - 2 * core) % planes, y, 1 - core),
        ctx_of(z, y, 1 - core),
        ctx_of(z, y + 1 - 2 * (y % 2), 1 - core),
    ):
        pl.semaphore_signal(barrier, inc=1, device_id=(other, x), device_id_type=MESH)
    lax.fori_loop(1, PLANE, one, 0)


def all_here():
    pl.semaphore_wait(pltpu.get_barrier_semaphore(), PLANE + 4)


def remote(src, dst, send, recv, ctx, x):
    return pltpu.make_async_remote_copy(
        src_ref=src, dst_ref=dst, send_sem=send, recv_sem=recv, device_id=(ctx, x), device_id_type=MESH
    )


def bring(
    planes,
    q_hbm,
    g_hbm,
    k_hbm,
    v_hbm,
    sel_hbm,
    qd_out,
    sel_out,
    store,
    acc,
    q,
    g,
    k,
    v,
    sel,
    qd,
    kv,
    sel_all,
    load_sem,
    near_send,
    near_recv,
    q_send,
    q_recv,
    i_send,
    i_recv,
    ring_send,
    ring_recv,
    pair_send,
    pair_recv,
    mate_send,
    mate_recv,
    over_send,
    over_recv,
    own_sem,
):
    x, y, z, core = place()
    half_way = planes // 2
    last = half_way - 1
    parity = y % 2
    mate = y + 1 - 2 * parity
    heads = q.shape[1]

    loads = [
        pltpu.make_async_copy(src, dst, load_sem.at[i])
        for i, (src, dst) in enumerate(
            ((k_hbm, k), (v_hbm, v), (q_hbm, q), (g_hbm, g), (sel_hbm, sel))
        )
    ]
    for copy in loads:
        copy.start()
    announce(planes, x, y, z, core)
    for copy in loads[:2]:
        copy.wait()
    for b in range(2):
        tokens = pl.ds(b * BLOCK, BLOCK)
        kv[:, b, 0] = jnp.swapaxes(k[tokens], 0, 1)
        kv[:, b, 1] = jnp.swapaxes(v[tokens], 0, 1)
    all_here()

    def near(d):
        to = (y + d) % SIDE
        return remote(
            kv.at[2 * x + to // 2],
            store.at[pl.ds(z * 16 + core * 8 + y * 2, 2)],
            near_send.at[d - 1],
            near_recv.at[d - 1],
            ctx_of(z, to, core),
            x,
        )

    def query(i):
        t = (x * SIDE + y + i) % PLANE
        return remote(
            qd.at[unit_of(t // SIDE, t % SIDE)],
            qd_out.at[x * SIDE + y],
            q_send.at[i - 1],
            q_recv.at[i - 1],
            ctx_of(z, t % SIDE, core),
            t // SIDE,
        )

    def index(d):
        return remote(
            sel, sel_all.at[x], i_send.at[d - 1], i_recv.at[d - 1], ctx_of(z, y, core), (x + d) % SIDE
        )

    way = 1 - 2 * core
    ahead = ctx_of((z + planes + way) % planes, y, core)
    partner = ctx_of(z, y, 1 - core)

    def piece(j, towards, side, row, count=2):
        origin = (z + planes - j * towards) % planes
        return store.at[pl.ds(origin * 16 + side * 8 + row, count)]

    def here(j, k, i):
        return piece(j, way, (core + k) % 2, 2 * piece_of(parity, i))

    def there(j, k, i):
        return piece(j, -way, (1 - core + k) % 2, 2 * piece_of(parity, i))

    def left_out(j, k):
        return piece(j, way, (core + k) % 2, 6 * (1 - parity))

    def hop(s, k, i):
        part = here(s - 1, k, i)
        return remote(part, part, ring_send.at[s - 1, k, i], ring_recv.at[s - 1, k, i], ahead, x)

    def arrived(j, k, i):
        part = here(j, k, i)
        return remote(part, part, ring_send.at[j - 1, k, i], ring_recv.at[j - 1, k, i], ahead, x)

    def share(j, k, i):
        part = here(j, k, i)
        return remote(part, part, pair_send.at[j - 1, k, i], pair_recv.at[j - 1, k, i], partner, x)

    def shared(j, k, i):
        part = there(j, k, i)
        return remote(part, part, pair_send.at[j - 1, k, i], pair_recv.at[j - 1, k, i], partner, x)

    def share_own(side):
        part = piece(0, 1, side, 0, 8)
        return remote(part, part, own_sem.at[1], own_sem.at[2], partner, x)

    def cross(j, k):
        part = here(j, k, 0)
        sems = mate_send.at[j - 1, k], mate_recv.at[j - 1, k]
        return remote(part, part, *sems, ctx_of(z, mate, core), x)

    def crossed(j, k):
        part = left_out(j, k)
        sems = mate_send.at[j - 1, k], mate_recv.at[j - 1, k]
        return remote(part, part, *sems, ctx_of(z, mate, core), x)

    def over(j, k):
        part = left_out(j, k)
        return remote(part, part, over_send.at[j - 1, k], over_recv.at[j - 1, k], partner, x)

    def overed(j, k):
        part = piece(j, -way, (1 - core + k) % 2, 6 * (1 - parity))
        return remote(part, part, over_send.at[j - 1, k], over_recv.at[j - 1, k], partner, x)

    def cross_over(row, side):
        part = piece(half_way, 1, side, row)
        sems = over_send.at[last, 0], over_recv.at[last, 0]
        return remote(part, part, *sems, ctx_of(z, mate, 1 - core), x)

    def first(i, row):
        part = piece(0, 1, core, row)
        return remote(part, part, ring_send.at[0, 0, i], ring_recv.at[0, 0, i], ahead, x)

    outer = 2 * (((y + 1) // 2) % 2)
    remote(
        kv.at[2 * x + y // 2],
        piece(0, 1, core, 2 * y),
        ring_send.at[0, 0, outer],
        ring_recv.at[0, 0, outer],
        ahead,
        x,
    ).start()
    for d in range(1, SIDE):
        near(d).start()
    mine = pltpu.make_async_copy(
        kv.at[2 * x + y // 2], store.at[pl.ds(z * 16 + core * 8 + y * 2, 2)], own_sem.at[0]
    )
    mine.start()
    for copy in loads[2:]:
        copy.wait()
    for d in range(1, SIDE):
        index(d).start()
    for b in range(2):
        tokens = pl.ds(b * BLOCK, BLOCK)
        units = pl.ds(b * heads, heads)
        qd[units, 0] = jnp.swapaxes(q[tokens], 0, 1)
        qd[units, 1] = jnp.swapaxes(g[tokens], 0, 1)
    mine.wait()
    for d in range(1, SIDE):
        near(d).wait_recv()
    first(2 - outer, 2 * (2 * parity + 2 - y)).start()
    first(1, 2 * (parity + 1)).start()
    share_own(core).start()

    def send_query(i, carry):
        query(i).start()
        return carry

    lax.fori_loop(1, PLANE, send_query, 0)
    qd_out[x * SIDE + y] = qd[unit_of(x, y)]
    sel_all[x] = sel[...]
    share_own(1 - core).wait_recv()
    for i in range(3):
        hop(1, 1, i).start()

    def clear(i, carry):
        acc[pl.ds(i * 4, 4)] = jnp.zeros((4, 2, BLOCK, HEAD), jnp.bfloat16)
        return carry

    lax.fori_loop(0, acc.shape[0] // 4, clear, 0)

    def step(s, carry):
        for k in range(2):
            for i in range(3):
                arrived(s - 1, k, i).wait_recv()
                hop(s, k, i).start()
                if i == 0:
                    cross(s - 1, k).start()
                share(s - 1, k, i).start()

        @pl.when(s > 2)
        def _():
            for k in range(2):
                crossed(s - 2, k).wait_recv()
                over(s - 2, k).start()

        return carry

    lax.fori_loop(2, half_way, step, 0)
    for k in range(2):
        for i in range(3):
            arrived(last, k, i).wait_recv()
            if k == 0:
                hop(half_way, 0, i).start()
            if i == 0:
                cross(last, k).start()
            share(last, k, i).start()
    for k in range(2):
        crossed(last - 1, k).wait_recv()
        over(last - 1, k).start()
    for i in range(3):
        arrived(half_way, 0, i).wait_recv()
        if i == 0:
            cross(half_way, 0).start()
            cross_over(6 * parity, core).start()
        share(half_way, 0, i).start()
    for k in range(2):
        crossed(last, k).wait_recv()
        over(last, k).start()

    def finish_query(i, carry):
        query(i).wait()
        return carry

    lax.fori_loop(1, PLANE, finish_query, 0)
    for d in range(1, SIDE):
        index(d).wait()
    own_head = lax.broadcasted_iota(jnp.int32, sel.shape, 1) == 2 * x + y // 2
    for group in range(SIDE):
        sel_out[group] = jnp.sum(jnp.where(own_head, sel_all[group], 0), axis=1)

    for d in range(1, SIDE):
        near(d).wait_send()
    share_own(core).wait_send()
    for i in range(3):
        hop(1, 0, i).wait_send()
        hop(1, 1, i).wait_send()

    def finish(j, carry):
        for k in range(2):
            for i in range(3):
                shared(j, k, i).wait_recv()
                share(j, k, i).wait_send()
            cross(j, k).wait_send()
            overed(j, k).wait_recv()
            over(j, k).wait_send()
        return carry

    lax.fori_loop(1, half_way, finish, 0)

    def finish_hop(s, carry):
        for k in range(2):
            for i in range(3):
                hop(s, k, i).wait_send()
        return carry

    lax.fori_loop(2, half_way, finish_hop, 0)
    for i in range(3):
        hop(half_way, 0, i).wait_send()
        shared(half_way, 0, i).wait_recv()
        share(half_way, 0, i).wait_send()
    cross(half_way, 0).wait_send()
    cross_over(6 * parity, core).wait_send()
    crossed(half_way, 0).wait_recv()
    cross_over(6 * (1 - parity), 1 - core).wait_recv()


def attend(sel, qd, store, cleared, od, acc):
    x, y, z, core = place()
    parity = y % 2
    factor = HEAD**-0.5
    rate = factor * math.log2(math.e)
    f32, bf16 = jnp.float32, jnp.bfloat16
    nt = (((1,), (1,)), ((), ()))
    nn = (((1,), (0,)), ((), ()))
    tn = (((0,), (0,)), ((), ()))

    def dot(a, b, dims):
        return lax.dot_general(a, b, dims, preferred_element_type=f32)

    def one(side, carry):
        own = z * 16 + core * 8 + side * 2 + parity
        block = ((z * SIDE + side) * 2 + core) * 2 + parity
        own_terms = [jnp.zeros((BLOCK, HEAD), f32)] * 2
        groups = range(SIDE)
        rows, keys, values = {}, {}, {}
        for group in groups:
            rows[group] = [own]
            for t in range(3):
                n = sel[group, t, block]
                rows[group].append(
                    (n // 16) * 16 + ((n // 2) % 2) * 8 + ((n // 4) % SIDE) * 2 + n % 2
                )
        for group in groups:
            keys[group] = jnp.concatenate([store[r, 0] for r in rows[group]], axis=0)
            values[group] = jnp.concatenate([store[r, 1] for r in rows[group]], axis=0)
        q = {group: qd[group * SIDE + side, 0] for group in groups}
        g = {group: qd[group * SIDE + side, 1] for group in groups}
        scores = {group: dot(q[group], keys[group], nt) for group in groups}
        grad_prob = {group: dot(g[group], values[group], nt) for group in groups}
        top = {group: jnp.max(scores[group], axis=1, keepdims=True) for group in groups}
        e = {group: jnp.exp2((scores[group] - top[group]) * rate) for group in groups}
        total = {group: jnp.sum(e[group], axis=1, keepdims=True) for group in groups}
        inverse = {group: 1.0 / total[group] for group in groups}
        prob_b = {group: (e[group] * inverse[group]).astype(bf16) for group in groups}
        scaled = {group: e[group] * (inverse[group] * factor) for group in groups}
        out = {group: dot(prob_b[group], values[group], nn).astype(bf16) for group in groups}
        value_terms = {group: dot(prob_b[group], g[group], tn) for group in groups}
        delta = {
            group: jnp.sum(g[group].astype(f32) * out[group].astype(f32), axis=1, keepdims=True)
            for group in groups
        }
        grad_scores = {
            group: (scaled[group] * (grad_prob[group] - delta[group])).astype(bf16)
            for group in groups
        }
        key_terms = {group: dot(grad_scores[group], q[group], tn) for group in groups}
        query_terms = {group: dot(grad_scores[group], keys[group], nn) for group in groups}
        for group in groups:
            u = group * SIDE + side
            od[u, 0] = out[group]
            od[u, 1] = query_terms[group].astype(bf16)
            for i, terms in enumerate((key_terms[group], value_terms[group])):
                own_terms[i] += terms[:BLOCK]
                for t in range(1, 4):
                    row = rows[group][t]
                    part = terms[t * BLOCK : (t + 1) * BLOCK]
                    acc[row, i] = (acc[row, i].astype(f32) + part).astype(bf16)
        for i in range(2):
            acc[own, i] = (acc[own, i].astype(f32) + own_terms[i]).astype(bf16)
        return carry

    lax.fori_loop(0, SIDE, one, 0)


def give(
    planes,
    od,
    acc,
    att,
    grad_q,
    kvg,
    part,
    inbox,
    outbox,
    mate_in,
    mate_out,
    fin,
    spread,
    od_all,
    q_send,
    q_recv,
    pair_send,
    pair_recv,
    mate_send,
    mate_recv,
    ring_send,
    ring_recv,
    near_send,
    near_recv,
    mine_sem,
):
    x, y, z, core = place()
    half_way = planes // 2
    parity = y % 2
    mate = y + 1 - 2 * parity
    heads = att.shape[1]
    f32, bf16 = jnp.float32, jnp.bfloat16

    announce(planes, x, y, z, core)
    for d in range(2):
        inbox[d, 0, 1, 1 - d] = jnp.zeros((2, BLOCK, HEAD), bf16)
    all_here()

    def chunk(d, s):
        far = half_way - s
        return (z + far) % planes if d == 0 else (z + planes - far) % planes

    def pair(at):
        return remote(
            acc.at[pl.ds(at * 16 + (1 - core) * 8, 8)],
            part.at[at],
            pair_send.at[at],
            pair_recv.at[at],
            ctx_of(z, y, 1 - core),
            x,
        )

    def cross(at):
        return remote(
            mate_out.at[at],
            mate_in.at[at],
            mate_send.at[at],
            mate_recv.at[at],
            ctx_of(z, mate, core),
            x,
        )

    def hop(d, s, i):
        to = (z + 1) % planes if d == 0 else (z + planes - 1) % planes
        box = (d, s, i, pl.ds(d, 1)) if isinstance(s, int) and s == 0 and i == 1 else (d, s, i)
        return remote(
            outbox.at[box],
            inbox.at[box],
            ring_send.at[d, s, i],
            ring_recv.at[d, s, i],
            ctx_of(to, y, core),
            x,
        )

    def answer(i):
        t = (x * SIDE + y + i) % PLANE
        return remote(
            od.at[t],
            od_all.at[unit_of(x, y)],
            q_send.at[i - 1],
            q_recv.at[i - 1],
            ctx_of(z, t % SIDE, core),
            t // SIDE,
        )

    def near(d):
        to = (y + d) % SIDE
        return remote(
            fin.at[pl.ds(to * 2, 2)],
            spread.at[y],
            near_send.at[d - 1],
            near_recv.at[d - 1],
            ctx_of(z, to, core),
            x,
        )

    def chip_sum(at, first, count):
        mine = acc[pl.ds(at * 16 + core * 8 + first, count)].astype(f32)
        return mine + part[at, pl.ds(first, count)].astype(f32)

    def prepare(at):
        pair(at).wait_recv()
        mate_out[at] = chip_sum(at, 6 * (1 - parity), 2).astype(bf16)
        cross(at).start()

    def emit(d, s, i, extra):
        at = chunk(d, s)
        total = chip_sum(at, 2 * piece_of(parity, i), 2)
        if i == 0:
            total += mate_in[at].astype(f32)
        if extra:
            hop(d, s - 1, i).wait_recv()
            total += inbox[d, s - 1, i].astype(f32)
        outbox[d, s, i] = total.astype(bf16)
        hop(d, s, i).start()

    pair(chunk(0, 0)).start()

    def begin_step(s, carry):
        pair(chunk(0, s)).start()
        pair(chunk(1, s)).start()
        return carry

    lax.fori_loop(1, half_way, begin_step, 0)
    pair(z).start()

    home = pltpu.make_async_copy(od.at[x * SIDE + y], od_all.at[unit_of(x, y)], mine_sem)
    home.start()

    def send_answer(i, carry):
        answer(i).start()
        return carry

    prepare(chunk(0, 0))
    for d in range(2):
        emit(d, 0, 1, False)
    emit(1, 0, 2, False)
    for d in range(2):
        prepare(chunk(d, 1))
    cross(chunk(0, 0)).wait_recv()
    emit(0, 0, 0, False)
    lax.fori_loop(1, PLANE, send_answer, 0)
    for d in range(2):
        prepare(chunk(d, 2))
    for i in (2, 1, 0):
        for d in range(2):
            if i == 0:
                cross(chunk(d, 1)).wait_recv()
            emit(d, 1, i, i in HALVES[d])

    def step(s, carry):
        @pl.when(s + 1 < half_way)
        def _():
            for d in range(2):
                prepare(chunk(d, s + 1))

        for i in (2, 1, 0):
            for d in range(2):
                if i == 0:
                    cross(chunk(d, s)).wait_recv()
                emit(d, s, i, True)
        return carry

    lax.fori_loop(2, half_way, step, 0)

    def scatter(to):
        @pl.when(to != y)
        def _():
            near((to + SIDE - y) % SIDE).start()

    pair(z).wait_recv()
    rest = 6 * (1 - parity)
    fin[pl.ds(rest, 2)] = chip_sum(z, rest, 2).astype(bf16)
    scatter(3 * (1 - parity))

    def finish_answer(i, carry):
        answer(i).wait()
        return carry

    lax.fori_loop(1, PLANE, finish_answer, 0)
    home.wait()
    for b in range(2):
        tokens = pl.ds(b * BLOCK, BLOCK)
        units = pl.ds(b * heads, heads)
        att[tokens] = jnp.swapaxes(od_all[units, 0], 0, 1)
        grad_q[tokens] = jnp.swapaxes(od_all[units, 1], 0, 1)

    for i in (2, 1, 0):
        first = 2 * piece_of(parity, i)
        total = chip_sum(z, first, 2)
        for d in range(2):
            hop(d, half_way - 1, i).wait_recv()
            total += inbox[d, half_way - 1, i].astype(f32)
        fin[pl.ds(first, 2)] = total.astype(bf16)
        scatter(piece_of(parity, i))
    spread[y] = fin[pl.ds(y * 2, 2)]

    def finish(s, carry):
        for d in range(2):
            for i in range(3):
                hop(d, s, i).wait_send()
            cross(chunk(d, s)).wait_send()
            pair(chunk(d, s)).wait_send()
        return carry

    lax.fori_loop(1, half_way, finish, 0)
    for d in range(2):
        for i in HALVES[d]:
            hop(d, 0, i).wait_send()
    cross(chunk(0, 0)).wait_send()
    pair(chunk(0, 0)).wait_send()
    pair(z).wait_send()

    for d in range(1, SIDE):
        near(d).wait()
    for pick in range(2):
        kvg[pick] = (spread[2 * pick].astype(f32) + spread[2 * pick + 1].astype(f32)).astype(bf16)


def leave(att, grad_q, kvg, att_out, grad_q_out, grad_k_out, grad_v_out, pair, sem):
    copies = [
        pltpu.make_async_copy(src, dst, sem.at[i])
        for i, (src, dst) in enumerate(
            (
                (att, att_out),
                (grad_q, grad_q_out),
                (pair.at[0], grad_k_out),
                (pair.at[1], grad_v_out),
            )
        )
    ]
    for copy in copies[:2]:
        copy.start()
    for b in range(2):
        for i in range(2):
            pair[i, pl.ds(b * BLOCK, BLOCK)] = jnp.swapaxes(kvg[:, b, i], 0, 1)
    for copy in copies[2:]:
        copy.start()
    for copy in copies:
        copy.wait()


def local(planes, queries, key_states, value_states, grad_out, selected):
    bf16 = jnp.bfloat16
    dma = pltpu.SemaphoreType.DMA
    half_way = planes // 2
    heads = queries.shape[1]
    blocks = selected.shape[0]

    shape = jax.ShapeDtypeStruct
    units = (PLANE, 2, BLOCK, HEAD)
    rows = (planes * 16, 2, BLOCK, HEAD)
    lists = (3, heads, blocks)
    given = queries, grad_out, key_states, value_states, selected.transpose(2, 1, 0)

    qd, sel, store, cleared = pl.pallas_call(
        functools.partial(bring, planes),
        name="bring",
        out_shape=(
            shape(units, bf16),
            shape((SIDE, 3, blocks), jnp.int32),
            shape(rows, bf16),
            shape(rows, bf16),
        ),
        in_specs=[HBM] * 5,
        out_specs=(VMEM,) * 4,
        scratch_shapes=[
            pltpu.VMEM(queries.shape, bf16),
            pltpu.VMEM(queries.shape, bf16),
            pltpu.VMEM(queries.shape, bf16),
            pltpu.VMEM(queries.shape, bf16),
            pltpu.VMEM(lists, jnp.int32),
            pltpu.VMEM(units, bf16),
            pltpu.VMEM((heads, 2, 2, BLOCK, HEAD), bf16),
            pltpu.VMEM((SIDE, *lists), jnp.int32),
            dma((5,)),
            dma((SIDE - 1,)),
            dma((SIDE - 1,)),
            dma((PLANE - 1,)),
            dma((PLANE - 1,)),
            dma((SIDE - 1,)),
            dma((SIDE - 1,)),
            dma((half_way, 2, 3)),
            dma((half_way, 2, 3)),
            dma((half_way, 2, 3)),
            dma((half_way, 2, 3)),
            dma((half_way, 2)),
            dma((half_way, 2)),
            dma((half_way, 2)),
            dma((half_way, 2)),
            dma((3,)),
        ],
        compiler_params=pltpu.CompilerParams(
            collective_id=0, has_side_effects=True, vmem_limit_bytes=16 * 1024 * 1024
        ),
    )(*(pltpu.with_memory_space_constraint(a, pltpu.HBM) for a in given))

    od, acc = pl.pallas_call(
        attend,
        name="attend",
        out_shape=(shape(units, bf16), shape(rows, bf16)),
        in_specs=[SMEM, VMEM, VMEM, VMEM],
        out_specs=(VMEM, VMEM),
        input_output_aliases={3: 1},
        compiler_params=pltpu.CompilerParams(vmem_limit_bytes=24 * 1024 * 1024),
    )(sel, qd, store, cleared)

    piece = (3, 2, 2, BLOCK, HEAD)
    att, grad_q, kvg = pl.pallas_call(
        functools.partial(give, planes),
        name="give",
        out_shape=(
            shape(queries.shape, bf16),
            shape(queries.shape, bf16),
            shape((2, 2, 2, BLOCK, HEAD), bf16),
        ),
        in_specs=[VMEM, VMEM],
        out_specs=(VMEM,) * 3,
        scratch_shapes=[
            pltpu.VMEM((planes, 8, 2, BLOCK, HEAD), bf16),
            pltpu.VMEM((2, half_way, *piece), bf16),
            pltpu.VMEM((2, half_way, *piece), bf16),
            pltpu.VMEM((planes, 2, 2, BLOCK, HEAD), bf16),
            pltpu.VMEM((planes, 2, 2, BLOCK, HEAD), bf16),
            pltpu.VMEM((8, 2, BLOCK, HEAD), bf16),
            pltpu.VMEM((SIDE, 2, 2, BLOCK, HEAD), bf16),
            pltpu.VMEM(units, bf16),
            dma((PLANE - 1,)),
            dma((PLANE - 1,)),
            dma((planes,)),
            dma((planes,)),
            dma((planes,)),
            dma((planes,)),
            dma((2, half_way, 3)),
            dma((2, half_way, 3)),
            dma((SIDE - 1,)),
            dma((SIDE - 1,)),
            dma,
        ],
        compiler_params=pltpu.CompilerParams(
            collective_id=1, has_side_effects=True, vmem_limit_bytes=28 * 1024 * 1024
        ),
    )(od, acc)

    key_shape = (2 * BLOCK, 2, HEAD)
    return pl.pallas_call(
        leave,
        name="leave",
        out_shape=(
            shape(queries.shape, bf16),
            shape(queries.shape, bf16),
            shape(key_shape, bf16),
            shape(key_shape, bf16),
        ),
        in_specs=[VMEM] * 3,
        out_specs=(HBM,) * 4,
        scratch_shapes=[pltpu.VMEM((2, *key_shape), bf16), dma((4,))],
        compiler_params=pltpu.CompilerParams(vmem_limit_bytes=4 * 1024 * 1024),
    )(att, grad_q, kvg)


def solution(mesh):
    planes = mesh.shape["ctx"] // (2 * SIDE)
    spread = P("ctx", "head", None)
    whole = P("ctx", None, None)
    return jax.shard_map(
        functools.partial(local, planes),
        mesh=mesh,
        in_specs=(spread, whole, whole, spread, P(None, "head", None)),
        out_specs=(spread, spread, spread, spread),
        check_vma=False,
    )
```

```python
import functools
import math

import jax
import jax.numpy as jnp
from jax import lax
from jax.experimental import pallas as pl
from jax.experimental.pallas import tpu as pltpu
from jax.sharding import PartitionSpec as P

BLOCK = 64
HEAD = 128
SIDE = 4
PLANE = SIDE * SIDE
MESH = pl.DeviceIdType.MESH
VMEM = pl.BlockSpec(memory_space=pltpu.VMEM)
SMEM = pl.BlockSpec(memory_space=pltpu.SMEM)
HBM = pl.BlockSpec(memory_space=pltpu.HBM)

HALVES = ((0, 1), (2, 1))


def place():
    ctx = lax.axis_index("ctx")
    x = lax.axis_index("head")
    return x, (ctx // 2) % SIDE, ctx // (2 * SIDE), ctx % 2


def ctx_of(z, y, core):
    return (z * SIDE + y) * 2 + core


def unit_of(x, y):
    return (y % 2) * 8 + 2 * x + y // 2


def piece_of(parity, i):
    return (3 * parity, parity + 1, 2 - parity)[i]


def announce(planes, x, y, z, core):
    barrier = pltpu.get_barrier_semaphore()

    def one(k, carry):
        t = (x * SIDE + y + k) % PLANE
        pl.semaphore_signal(
            barrier, inc=1, device_id=(ctx_of(z, t % SIDE, core), t // SIDE), device_id_type=MESH
        )
        return carry

    for other in (
        ctx_of((z + 1) % planes, y, core),
        ctx_of((z + planes - 1) % planes, y, core),
        ctx_of((z + planes + 1 - 2 * core) % planes, y, 1 - core),
        ctx_of(z, y, 1 - core),
        ctx_of(z, y + 1 - 2 * (y % 2), 1 - core),
    ):
        pl.semaphore_signal(barrier, inc=1, device_id=(other, x), device_id_type=MESH)
    lax.fori_loop(1, PLANE, one, 0)


def all_here():
    pl.semaphore_wait(pltpu.get_barrier_semaphore(), PLANE + 4)


def remote(src, dst, send, recv, ctx, x):
    return pltpu.make_async_remote_copy(
        src_ref=src, dst_ref=dst, send_sem=send, recv_sem=recv, device_id=(ctx, x), device_id_type=MESH
    )


def bring(
    planes,
    q_hbm,
    g_hbm,
    k_hbm,
    v_hbm,
    sel_hbm,
    qd_out,
    sel_out,
    store,
    acc,
    q,
    g,
    k,
    v,
    sel,
    qd,
    kv,
    sel_all,
    load_sem,
    near_send,
    near_recv,
    q_send,
    q_recv,
    i_send,
    i_recv,
    ring_send,
    ring_recv,
    pair_send,
    pair_recv,
    mate_send,
    mate_recv,
    over_send,
    over_recv,
    own_sem,
):
    x, y, z, core = place()
    half_way = planes // 2
    last = half_way - 1
    parity = y % 2
    mate = y + 1 - 2 * parity
    heads = q.shape[1]

    loads = [
        pltpu.make_async_copy(src, dst, load_sem.at[i])
        for i, (src, dst) in enumerate(
            ((k_hbm, k), (v_hbm, v), (q_hbm, q), (g_hbm, g), (sel_hbm, sel))
        )
    ]
    for copy in loads:
        copy.start()
    announce(planes, x, y, z, core)
    for copy in loads[:2]:
        copy.wait()
    for b in range(2):
        tokens = pl.ds(b * BLOCK, BLOCK)
        kv[:, b, 0] = jnp.swapaxes(k[tokens], 0, 1)
        kv[:, b, 1] = jnp.swapaxes(v[tokens], 0, 1)
    all_here()

    def near(d):
        to = (y + d) % SIDE
        return remote(
            kv.at[2 * x + to // 2],
            store.at[pl.ds(z * 16 + core * 8 + y * 2, 2)],
            near_send.at[d - 1],
            near_recv.at[d - 1],
            ctx_of(z, to, core),
            x,
        )

    def query(i):
        t = (x * SIDE + y + i) % PLANE
        return remote(
            qd.at[unit_of(t // SIDE, t % SIDE)],
            qd_out.at[x * SIDE + y],
            q_send.at[i - 1],
            q_recv.at[i - 1],
            ctx_of(z, t % SIDE, core),
            t // SIDE,
        )

    def index(d):
        return remote(
            sel, sel_all.at[x], i_send.at[d - 1], i_recv.at[d - 1], ctx_of(z, y, core), (x + d) % SIDE
        )

    way = 1 - 2 * core
    ahead = ctx_of((z + planes + way) % planes, y, core)
    partner = ctx_of(z, y, 1 - core)

    def piece(j, towards, side, row, count=2):
        origin = (z + planes - j * towards) % planes
        return store.at[pl.ds(origin * 16 + side * 8 + row, count)]

    def here(j, k, i):
        return piece(j, way, (core + k) % 2, 2 * piece_of(parity, i))

    def there(j, k, i):
        return piece(j, -way, (1 - core + k) % 2, 2 * piece_of(parity, i))

    def left_out(j, k):
        return piece(j, way, (core + k) % 2, 6 * (1 - parity))

    def hop(s, k, i):
        part = here(s - 1, k, i)
        return remote(part, part, ring_send.at[s - 1, k, i], ring_recv.at[s - 1, k, i], ahead, x)

    def arrived(j, k, i):
        part = here(j, k, i)
        return remote(part, part, ring_send.at[j - 1, k, i], ring_recv.at[j - 1, k, i], ahead, x)

    def share(j, k, i):
        part = here(j, k, i)
        return remote(part, part, pair_send.at[j - 1, k, i], pair_recv.at[j - 1, k, i], partner, x)

    def shared(j, k, i):
        part = there(j, k, i)
        return remote(part, part, pair_send.at[j - 1, k, i], pair_recv.at[j - 1, k, i], partner, x)

    def share_own(side):
        part = piece(0, 1, side, 0, 8)
        return remote(part, part, own_sem.at[1], own_sem.at[2], partner, x)

    def cross(j, k):
        part = here(j, k, 0)
        sems = mate_send.at[j - 1, k], mate_recv.at[j - 1, k]
        return remote(part, part, *sems, ctx_of(z, mate, core), x)

    def crossed(j, k):
        part = left_out(j, k)
        sems = mate_send.at[j - 1, k], mate_recv.at[j - 1, k]
        return remote(part, part, *sems, ctx_of(z, mate, core), x)

    def over(j, k):
        part = left_out(j, k)
        return remote(part, part, over_send.at[j - 1, k], over_recv.at[j - 1, k], partner, x)

    def overed(j, k):
        part = piece(j, -way, (1 - core + k) % 2, 6 * (1 - parity))
        return remote(part, part, over_send.at[j - 1, k], over_recv.at[j - 1, k], partner, x)

    def cross_over(row, side):
        part = piece(half_way, 1, side, row)
        sems = over_send.at[last, 0], over_recv.at[last, 0]
        return remote(part, part, *sems, ctx_of(z, mate, 1 - core), x)

    def first(i, row):
        part = piece(0, 1, core, row)
        return remote(part, part, ring_send.at[0, 0, i], ring_recv.at[0, 0, i], ahead, x)

    outer = 2 * (((y + 1) // 2) % 2)
    remote(
        kv.at[2 * x + y // 2],
        piece(0, 1, core, 2 * y),
        ring_send.at[0, 0, outer],
        ring_recv.at[0, 0, outer],
        ahead,
        x,
    ).start()
    for d in range(1, SIDE):
        near(d).start()
    mine = pltpu.make_async_copy(
        kv.at[2 * x + y // 2], store.at[pl.ds(z * 16 + core * 8 + y * 2, 2)], own_sem.at[0]
    )
    mine.start()
    for copy in loads[2:]:
        copy.wait()
    for d in range(1, SIDE):
        index(d).start()
    for b in range(2):
        tokens = pl.ds(b * BLOCK, BLOCK)
        units = pl.ds(b * heads, heads)
        qd[units, 0] = jnp.swapaxes(q[tokens], 0, 1)
        qd[units, 1] = jnp.swapaxes(g[tokens], 0, 1)
    mine.wait()
    for d in range(1, SIDE):
        near(d).wait_recv()
    first(2 - outer, 2 * (2 * parity + 2 - y)).start()
    first(1, 2 * (parity + 1)).start()
    share_own(core).start()

    def send_query(i, carry):
        query(i).start()
        return carry

    lax.fori_loop(1, PLANE, send_query, 0)
    qd_out[x * SIDE + y] = qd[unit_of(x, y)]
    sel_all[x] = sel[...]
    share_own(1 - core).wait_recv()
    for i in range(3):
        hop(1, 1, i).start()

    def clear(i, carry):
        acc[pl.ds(i * 4, 4)] = jnp.zeros((4, 2, BLOCK, HEAD), jnp.bfloat16)
        return carry

    lax.fori_loop(0, acc.shape[0] // 4, clear, 0)

    def retire(j):
        for k in range(2):
            for i in range(3):
                hop(j, k, i).wait_send()
                shared(j, k, i).wait_recv()
                share(j, k, i).wait_send()
            cross(j, k).wait_send()
            overed(j, k).wait_recv()
            over(j, k).wait_send()

    def step(s, carry):
        for k in range(2):
            for i in range(3):
                arrived(s - 1, k, i).wait_recv()
                hop(s, k, i).start()
                if i == 0:
                    cross(s - 1, k).start()
                share(s - 1, k, i).start()

        @pl.when(s > 2)
        def _():
            for k in range(2):
                crossed(s - 2, k).wait_recv()
                over(s - 2, k).start()

        @pl.when(s > 4)
        def _():
            retire(s - 4)

        return carry

    lax.fori_loop(2, half_way, step, 0)
    def finish_query(i, carry):
        query(i).wait()
        return carry

    lax.fori_loop(1, PLANE, finish_query, 0)
    for d in range(1, SIDE):
        index(d).wait()
    own_head = lax.broadcasted_iota(jnp.int32, sel.shape, 1) == 2 * x + y // 2
    for group in range(SIDE):
        sel_out[group] = jnp.sum(jnp.where(own_head, sel_all[group], 0), axis=1)
    for d in range(1, SIDE):
        near(d).wait_send()
    share_own(core).wait_send()
    retire(last - 3)
    for k in range(2):
        for i in range(3):
            arrived(last, k, i).wait_recv()
            if k == 0:
                hop(half_way, 0, i).start()
            if i == 0:
                cross(last, k).start()
            share(last, k, i).start()
    for k in range(2):
        crossed(last - 1, k).wait_recv()
        over(last - 1, k).start()
    retire(last - 2)
    for i in range(3):
        arrived(half_way, 0, i).wait_recv()
        if i == 0:
            cross(half_way, 0).start()
            cross_over(6 * parity, core).start()
        share(half_way, 0, i).start()
    for k in range(2):
        crossed(last, k).wait_recv()
        over(last, k).start()

    retire(last - 1)
    retire(last)
    for i in range(3):
        hop(half_way, 0, i).wait_send()
        shared(half_way, 0, i).wait_recv()
        share(half_way, 0, i).wait_send()
    cross(half_way, 0).wait_send()
    cross_over(6 * parity, core).wait_send()
    crossed(half_way, 0).wait_recv()
    cross_over(6 * (1 - parity), 1 - core).wait_recv()


def attend(sel, qd, store, cleared, od, acc):
    x, y, z, core = place()
    parity = y % 2
    factor = HEAD**-0.5
    rate = factor * math.log2(math.e)
    f32, bf16 = jnp.float32, jnp.bfloat16
    nt = (((1,), (1,)), ((), ()))
    nn = (((1,), (0,)), ((), ()))
    tn = (((0,), (0,)), ((), ()))

    def dot(a, b, dims):
        return lax.dot_general(a, b, dims, preferred_element_type=f32)

    def one(side, carry):
        own = z * 16 + core * 8 + side * 2 + parity
        block = ((z * SIDE + side) * 2 + core) * 2 + parity
        own_terms = [jnp.zeros((BLOCK, HEAD), f32)] * 2
        groups = range(SIDE)
        rows, keys, values = {}, {}, {}
        for group in groups:
            rows[group] = [own]
            for t in range(3):
                n = sel[group, t, block]
                rows[group].append(
                    (n // 16) * 16 + ((n // 2) % 2) * 8 + ((n // 4) % SIDE) * 2 + n % 2
                )
        for group in groups:
            keys[group] = jnp.concatenate([store[r, 0] for r in rows[group]], axis=0)
            values[group] = jnp.concatenate([store[r, 1] for r in rows[group]], axis=0)
        q = {group: qd[group * SIDE + side, 0] for group in groups}
        g = {group: qd[group * SIDE + side, 1] for group in groups}
        scores = {group: dot(q[group], keys[group], nt) for group in groups}
        grad_prob = {group: dot(g[group], values[group], nt) for group in groups}
        top = {group: jnp.max(scores[group], axis=1, keepdims=True) for group in groups}
        e = {group: jnp.exp2((scores[group] - top[group]) * rate) for group in groups}
        total = {group: jnp.sum(e[group], axis=1, keepdims=True) for group in groups}
        inverse = {group: 1.0 / total[group] for group in groups}
        prob_b = {group: (e[group] * inverse[group]).astype(bf16) for group in groups}
        scaled = {group: e[group] * (inverse[group] * factor) for group in groups}
        out = {group: dot(prob_b[group], values[group], nn).astype(bf16) for group in groups}
        value_terms = {group: dot(prob_b[group], g[group], tn) for group in groups}
        delta = {
            group: jnp.sum(g[group].astype(f32) * out[group].astype(f32), axis=1, keepdims=True)
            for group in groups
        }
        grad_scores = {
            group: (scaled[group] * (grad_prob[group] - delta[group])).astype(bf16)
            for group in groups
        }
        key_terms = {group: dot(grad_scores[group], q[group], tn) for group in groups}
        query_terms = {group: dot(grad_scores[group], keys[group], nn) for group in groups}
        for group in groups:
            u = group * SIDE + side
            od[u, 0] = out[group]
            od[u, 1] = query_terms[group].astype(bf16)
            for i, terms in enumerate((key_terms[group], value_terms[group])):
                own_terms[i] += terms[:BLOCK]
                for t in range(1, 4):
                    row = rows[group][t]
                    part = terms[t * BLOCK : (t + 1) * BLOCK]
                    acc[row, i] = (acc[row, i].astype(f32) + part).astype(bf16)
        for i in range(2):
            acc[own, i] = (acc[own, i].astype(f32) + own_terms[i]).astype(bf16)
        return carry

    lax.fori_loop(0, SIDE, one, 0)


def give(
    planes,
    od,
    acc,
    att,
    grad_q,
    kvg,
    part,
    inbox,
    outbox,
    mate_in,
    mate_out,
    fin,
    spread,
    od_all,
    q_send,
    q_recv,
    pair_send,
    pair_recv,
    mate_send,
    mate_recv,
    ring_send,
    ring_recv,
    near_send,
    near_recv,
    mine_sem,
):
    x, y, z, core = place()
    half_way = planes // 2
    parity = y % 2
    mate = y + 1 - 2 * parity
    heads = att.shape[1]
    f32, bf16 = jnp.float32, jnp.bfloat16

    announce(planes, x, y, z, core)
    for d in range(2):
        inbox[d, 0, 1, 1 - d] = jnp.zeros((2, BLOCK, HEAD), bf16)
    all_here()

    def chunk(d, s):
        far = half_way - s
        return (z + far) % planes if d == 0 else (z + planes - far) % planes

    def pair(at):
        return remote(
            acc.at[pl.ds(at * 16 + (1 - core) * 8, 8)],
            part.at[at],
            pair_send.at[at],
            pair_recv.at[at],
            ctx_of(z, y, 1 - core),
            x,
        )

    def cross(at):
        return remote(
            mate_out.at[at],
            mate_in.at[at],
            mate_send.at[at],
            mate_recv.at[at],
            ctx_of(z, mate, core),
            x,
        )

    def hop(d, s, i):
        to = (z + 1) % planes if d == 0 else (z + planes - 1) % planes
        box = (d, s, i, pl.ds(d, 1)) if isinstance(s, int) and s == 0 and i == 1 else (d, s, i)
        return remote(
            outbox.at[box],
            inbox.at[box],
            ring_send.at[d, s, i],
            ring_recv.at[d, s, i],
            ctx_of(to, y, core),
            x,
        )

    def answer(i):
        t = (x * SIDE + y + i) % PLANE
        return remote(
            od.at[t],
            od_all.at[unit_of(x, y)],
            q_send.at[i - 1],
            q_recv.at[i - 1],
            ctx_of(z, t % SIDE, core),
            t // SIDE,
        )

    def near(d):
        to = (y + d) % SIDE
        return remote(
            fin.at[pl.ds(to * 2, 2)],
            spread.at[y],
            near_send.at[d - 1],
            near_recv.at[d - 1],
            ctx_of(z, to, core),
            x,
        )

    def chip_sum(at, first, count):
        mine = acc[pl.ds(at * 16 + core * 8 + first, count)].astype(f32)
        return mine + part[at, pl.ds(first, count)].astype(f32)

    def prepare(at):
        pair(at).wait_recv()
        mate_out[at] = chip_sum(at, 6 * (1 - parity), 2).astype(bf16)
        cross(at).start()

    def emit(d, s, i, extra):
        at = chunk(d, s)
        total = chip_sum(at, 2 * piece_of(parity, i), 2)
        if i == 0:
            total += mate_in[at].astype(f32)
        if extra:
            hop(d, s - 1, i).wait_recv()
            total += inbox[d, s - 1, i].astype(f32)
        outbox[d, s, i] = total.astype(bf16)
        hop(d, s, i).start()

    pair(chunk(0, 0)).start()

    def begin_step(s, carry):
        pair(chunk(0, s)).start()
        pair(chunk(1, s)).start()
        return carry

    lax.fori_loop(1, half_way, begin_step, 0)
    pair(z).start()

    home = pltpu.make_async_copy(od.at[x * SIDE + y], od_all.at[unit_of(x, y)], mine_sem)
    home.start()

    prepare(chunk(0, 0))
    for d in range(2):
        emit(d, 0, 1, False)
    emit(1, 0, 2, False)
    for d in range(2):
        prepare(chunk(d, 1))
    cross(chunk(0, 0)).wait_recv()
    emit(0, 0, 0, False)
    for d in range(2):
        prepare(chunk(d, 2))
    for i in (2, 1, 0):
        for d in range(2):
            if i == 0:
                cross(chunk(d, 1)).wait_recv()
            emit(d, 1, i, i in HALVES[d])

    each = (PLANE - 1) // (half_way - 3)

    def step(s, carry):
        @pl.when(s + 1 < half_way)
        def _():
            for d in range(2):
                prepare(chunk(d, s + 1))
            for i in range(1, 1 + each):
                answer((s - 2) * each + i).start()

        for i in (2, 1, 0):
            for d in range(2):
                if i == 0:
                    cross(chunk(d, s)).wait_recv()
                emit(d, s, i, True)
        return carry

    lax.fori_loop(2, half_way, step, 0)

    def scatter(to):
        @pl.when(to != y)
        def _():
            near((to + SIDE - y) % SIDE).start()

    pair(z).wait_recv()
    rest = 6 * (1 - parity)
    fin[pl.ds(rest, 2)] = chip_sum(z, rest, 2).astype(bf16)
    scatter(3 * (1 - parity))

    def finish_answer(i, carry):
        answer(i).wait()
        return carry

    lax.fori_loop(1, PLANE, finish_answer, 0)
    home.wait()
    for b in range(2):
        tokens = pl.ds(b * BLOCK, BLOCK)
        units = pl.ds(b * heads, heads)
        att[tokens] = jnp.swapaxes(od_all[units, 0], 0, 1)
        grad_q[tokens] = jnp.swapaxes(od_all[units, 1], 0, 1)

    for i in (2, 1, 0):
        first = 2 * piece_of(parity, i)
        total = chip_sum(z, first, 2)
        for d in range(2):
            hop(d, half_way - 1, i).wait_recv()
            total += inbox[d, half_way - 1, i].astype(f32)
        fin[pl.ds(first, 2)] = total.astype(bf16)
        scatter(piece_of(parity, i))
    spread[y] = fin[pl.ds(y * 2, 2)]

    def finish(s, carry):
        for d in range(2):
            for i in range(3):
                hop(d, s, i).wait_send()
            cross(chunk(d, s)).wait_send()
            pair(chunk(d, s)).wait_send()
        return carry

    lax.fori_loop(1, half_way, finish, 0)
    for d in range(2):
        for i in HALVES[d]:
            hop(d, 0, i).wait_send()
    cross(chunk(0, 0)).wait_send()
    pair(chunk(0, 0)).wait_send()
    pair(z).wait_send()

    for d in range(1, SIDE):
        near(d).wait()
    for pick in range(2):
        kvg[pick] = (spread[2 * pick].astype(f32) + spread[2 * pick + 1].astype(f32)).astype(bf16)


def leave(att, grad_q, kvg, att_out, grad_q_out, grad_k_out, grad_v_out, pair, sem):
    copies = [
        pltpu.make_async_copy(src, dst, sem.at[i])
        for i, (src, dst) in enumerate(
            (
                (att, att_out),
                (grad_q, grad_q_out),
                (pair.at[0], grad_k_out),
                (pair.at[1], grad_v_out),
            )
        )
    ]
    for copy in copies[:2]:
        copy.start()
    for b in range(2):
        for i in range(2):
            pair[i, pl.ds(b * BLOCK, BLOCK)] = jnp.swapaxes(kvg[:, b, i], 0, 1)
    for copy in copies[2:]:
        copy.start()
    for copy in copies:
        copy.wait()


def local(planes, queries, key_states, value_states, grad_out, selected):
    bf16 = jnp.bfloat16
    dma = pltpu.SemaphoreType.DMA
    half_way = planes // 2
    heads = queries.shape[1]
    blocks = selected.shape[0]

    shape = jax.ShapeDtypeStruct
    units = (PLANE, 2, BLOCK, HEAD)
    rows = (planes * 16, 2, BLOCK, HEAD)
    lists = (3, heads, blocks)
    given = queries, grad_out, key_states, value_states, selected.transpose(2, 1, 0)

    qd, sel, store, cleared = pl.pallas_call(
        functools.partial(bring, planes),
        name="bring",
        out_shape=(
            shape(units, bf16),
            shape((SIDE, 3, blocks), jnp.int32),
            shape(rows, bf16),
            shape(rows, bf16),
        ),
        in_specs=[HBM] * 5,
        out_specs=(VMEM,) * 4,
        scratch_shapes=[
            pltpu.VMEM(queries.shape, bf16),
            pltpu.VMEM(queries.shape, bf16),
            pltpu.VMEM(queries.shape, bf16),
            pltpu.VMEM(queries.shape, bf16),
            pltpu.VMEM(lists, jnp.int32),
            pltpu.VMEM(units, bf16),
            pltpu.VMEM((heads, 2, 2, BLOCK, HEAD), bf16),
            pltpu.VMEM((SIDE, *lists), jnp.int32),
            dma((5,)),
            dma((SIDE - 1,)),
            dma((SIDE - 1,)),
            dma((PLANE - 1,)),
            dma((PLANE - 1,)),
            dma((SIDE - 1,)),
            dma((SIDE - 1,)),
            dma((half_way, 2, 3)),
            dma((half_way, 2, 3)),
            dma((half_way, 2, 3)),
            dma((half_way, 2, 3)),
            dma((half_way, 2)),
            dma((half_way, 2)),
            dma((half_way, 2)),
            dma((half_way, 2)),
            dma((3,)),
        ],
        compiler_params=pltpu.CompilerParams(
            collective_id=0, has_side_effects=True, vmem_limit_bytes=16 * 1024 * 1024
        ),
    )(*(pltpu.with_memory_space_constraint(a, pltpu.HBM) for a in given))

    od, acc = pl.pallas_call(
        attend,
        name="attend",
        out_shape=(shape(units, bf16), shape(rows, bf16)),
        in_specs=[SMEM, VMEM, VMEM, VMEM],
        out_specs=(VMEM, VMEM),
        input_output_aliases={3: 1},
        compiler_params=pltpu.CompilerParams(vmem_limit_bytes=24 * 1024 * 1024),
    )(sel, qd, store, cleared)

    piece = (3, 2, 2, BLOCK, HEAD)
    att, grad_q, kvg = pl.pallas_call(
        functools.partial(give, planes),
        name="give",
        out_shape=(
            shape(queries.shape, bf16),
            shape(queries.shape, bf16),
            shape((2, 2, 2, BLOCK, HEAD), bf16),
        ),
        in_specs=[VMEM, VMEM],
        out_specs=(VMEM,) * 3,
        scratch_shapes=[
            pltpu.VMEM((planes, 8, 2, BLOCK, HEAD), bf16),
            pltpu.VMEM((2, half_way, *piece), bf16),
            pltpu.VMEM((2, half_way, *piece), bf16),
            pltpu.VMEM((planes, 2, 2, BLOCK, HEAD), bf16),
            pltpu.VMEM((planes, 2, 2, BLOCK, HEAD), bf16),
            pltpu.VMEM((8, 2, BLOCK, HEAD), bf16),
            pltpu.VMEM((SIDE, 2, 2, BLOCK, HEAD), bf16),
            pltpu.VMEM(units, bf16),
            dma((PLANE - 1,)),
            dma((PLANE - 1,)),
            dma((planes,)),
            dma((planes,)),
            dma((planes,)),
            dma((planes,)),
            dma((2, half_way, 3)),
            dma((2, half_way, 3)),
            dma((SIDE - 1,)),
            dma((SIDE - 1,)),
            dma,
        ],
        compiler_params=pltpu.CompilerParams(
            collective_id=1, has_side_effects=True, vmem_limit_bytes=28 * 1024 * 1024
        ),
    )(od, acc)

    key_shape = (2 * BLOCK, 2, HEAD)
    return pl.pallas_call(
        leave,
        name="leave",
        out_shape=(
            shape(queries.shape, bf16),
            shape(queries.shape, bf16),
            shape(key_shape, bf16),
            shape(key_shape, bf16),
        ),
        in_specs=[VMEM] * 3,
        out_specs=(HBM,) * 4,
        scratch_shapes=[pltpu.VMEM((2, *key_shape), bf16), dma((4,))],
        compiler_params=pltpu.CompilerParams(vmem_limit_bytes=4 * 1024 * 1024),
    )(att, grad_q, kvg)


def solution(mesh):
    planes = mesh.shape["ctx"] // (2 * SIDE)
    spread = P("ctx", "head", None)
    whole = P("ctx", None, None)
    return jax.shard_map(
        functools.partial(local, planes),
        mesh=mesh,
        in_specs=(spread, whole, whole, spread, P(None, "head", None)),
        out_specs=(spread, spread, spread, spread),
        check_vma=False,
    )
```

```python
import functools
import math

import jax
import jax.numpy as jnp
from jax import lax
from jax.experimental import pallas as pl
from jax.experimental.pallas import tpu as pltpu
from jax.sharding import PartitionSpec as P

BLOCK = 64
HEAD = 128
SIDE = 4
PLANE = SIDE * SIDE
MESH = pl.DeviceIdType.MESH
VMEM = pl.BlockSpec(memory_space=pltpu.VMEM)
SMEM = pl.BlockSpec(memory_space=pltpu.SMEM)
HBM = pl.BlockSpec(memory_space=pltpu.HBM)

HALVES = ((0, 1), (2, 1))


def place():
    ctx = lax.axis_index("ctx")
    x = lax.axis_index("head")
    return x, (ctx // 2) % SIDE, ctx // (2 * SIDE), ctx % 2


def ctx_of(z, y, core):
    return (z * SIDE + y) * 2 + core


def unit_of(x, y):
    return (y % 2) * 8 + 2 * x + y // 2


def piece_of(parity, i):
    return (3 * parity, parity + 1, 2 - parity)[i]


def announce(planes, x, y, z, core):
    barrier = pltpu.get_barrier_semaphore()

    def one(k, carry):
        t = (x * SIDE + y + k) % PLANE
        pl.semaphore_signal(
            barrier, inc=1, device_id=(ctx_of(z, t % SIDE, core), t // SIDE), device_id_type=MESH
        )
        return carry

    for other in (
        ctx_of((z + 1) % planes, y, core),
        ctx_of((z + planes - 1) % planes, y, core),
        ctx_of((z + planes + 1 - 2 * core) % planes, y, 1 - core),
        ctx_of(z, y, 1 - core),
        ctx_of(z, y + 1 - 2 * (y % 2), 1 - core),
    ):
        pl.semaphore_signal(barrier, inc=1, device_id=(other, x), device_id_type=MESH)
    lax.fori_loop(1, PLANE, one, 0)


def all_here():
    pl.semaphore_wait(pltpu.get_barrier_semaphore(), PLANE + 4)


def remote(src, dst, send, recv, ctx, x):
    return pltpu.make_async_remote_copy(
        src_ref=src, dst_ref=dst, send_sem=send, recv_sem=recv, device_id=(ctx, x), device_id_type=MESH
    )


def bring(
    planes,
    q_hbm,
    g_hbm,
    k_hbm,
    v_hbm,
    sel_hbm,
    qd_out,
    sel_out,
    store,
    acc,
    q,
    g,
    k,
    v,
    sel,
    qd,
    kv,
    sel_all,
    load_sem,
    near_send,
    near_recv,
    q_send,
    q_recv,
    i_send,
    i_recv,
    ring_send,
    ring_recv,
    pair_send,
    pair_recv,
    mate_send,
    mate_recv,
    over_send,
    over_recv,
    own_sem,
):
    x, y, z, core = place()
    half_way = planes // 2
    last = half_way - 1
    parity = y % 2
    mate = y + 1 - 2 * parity
    heads = q.shape[1]

    loads = [
        pltpu.make_async_copy(src, dst, load_sem.at[i])
        for i, (src, dst) in enumerate(
            ((k_hbm, k), (v_hbm, v), (q_hbm, q), (g_hbm, g), (sel_hbm, sel))
        )
    ]
    for copy in loads:
        copy.start()
    announce(planes, x, y, z, core)
    for copy in loads[:2]:
        copy.wait()
    for b in range(2):
        tokens = pl.ds(b * BLOCK, BLOCK)
        kv[:, b, 0] = jnp.swapaxes(k[tokens], 0, 1)
        kv[:, b, 1] = jnp.swapaxes(v[tokens], 0, 1)
    all_here()

    def near(d):
        to = (y + d) % SIDE
        return remote(
            kv.at[2 * x + to // 2],
            store.at[pl.ds(z * 16 + core * 8 + y * 2, 2)],
            near_send.at[d - 1],
            near_recv.at[d - 1],
            ctx_of(z, to, core),
            x,
        )

    def query(i):
        t = (x * SIDE + y + i) % PLANE
        return remote(
            qd.at[unit_of(t // SIDE, t % SIDE)],
            qd_out.at[x * SIDE + y],
            q_send.at[i - 1],
            q_recv.at[i - 1],
            ctx_of(z, t % SIDE, core),
            t // SIDE,
        )

    def index(d):
        return remote(
            sel, sel_all.at[x], i_send.at[d - 1], i_recv.at[d - 1], ctx_of(z, y, core), (x + d) % SIDE
        )

    way = 1 - 2 * core
    ahead = ctx_of((z + planes + way) % planes, y, core)
    partner = ctx_of(z, y, 1 - core)

    def piece(j, towards, side, row, count=2):
        origin = (z + planes - j * towards) % planes
        return store.at[pl.ds(origin * 16 + side * 8 + row, count)]

    def here(j, k, i):
        return piece(j, way, (core + k) % 2, 2 * piece_of(parity, i))

    def there(j, k, i):
        return piece(j, -way, (1 - core + k) % 2, 2 * piece_of(parity, i))

    def left_out(j, k):
        return piece(j, way, (core + k) % 2, 6 * (1 - parity))

    def hop(s, k, i):
        part = here(s - 1, k, i)
        return remote(part, part, ring_send.at[s - 1, k, i], ring_recv.at[s - 1, k, i], ahead, x)

    def arrived(j, k, i):
        part = here(j, k, i)
        return remote(part, part, ring_send.at[j - 1, k, i], ring_recv.at[j - 1, k, i], ahead, x)

    def share(j, k, i):
        part = here(j, k, i)
        return remote(part, part, pair_send.at[j - 1, k, i], pair_recv.at[j - 1, k, i], partner, x)

    def shared(j, k, i):
        part = there(j, k, i)
        return remote(part, part, pair_send.at[j - 1, k, i], pair_recv.at[j - 1, k, i], partner, x)

    def share_own(side):
        part = piece(0, 1, side, 0, 8)
        return remote(part, part, own_sem.at[1], own_sem.at[2], partner, x)

    def cross(j, k):
        part = here(j, k, 0)
        sems = mate_send.at[j - 1, k], mate_recv.at[j - 1, k]
        return remote(part, part, *sems, ctx_of(z, mate, core), x)

    def crossed(j, k):
        part = left_out(j, k)
        sems = mate_send.at[j - 1, k], mate_recv.at[j - 1, k]
        return remote(part, part, *sems, ctx_of(z, mate, core), x)

    def over(j, k):
        part = left_out(j, k)
        return remote(part, part, over_send.at[j - 1, k], over_recv.at[j - 1, k], partner, x)

    def overed(j, k):
        part = piece(j, -way, (1 - core + k) % 2, 6 * (1 - parity))
        return remote(part, part, over_send.at[j - 1, k], over_recv.at[j - 1, k], partner, x)

    def cross_over(row, side):
        part = piece(half_way, 1, side, row)
        sems = over_send.at[last, 0], over_recv.at[last, 0]
        return remote(part, part, *sems, ctx_of(z, mate, 1 - core), x)

    def first(i, row):
        part = piece(0, 1, core, row)
        return remote(part, part, ring_send.at[0, 0, i], ring_recv.at[0, 0, i], ahead, x)

    outer = 2 * (((y + 1) // 2) % 2)
    remote(
        kv.at[2 * x + y // 2],
        piece(0, 1, core, 2 * y),
        ring_send.at[0, 0, outer],
        ring_recv.at[0, 0, outer],
        ahead,
        x,
    ).start()
    for d in range(1, SIDE):
        near(d).start()
    mine = pltpu.make_async_copy(
        kv.at[2 * x + y // 2], store.at[pl.ds(z * 16 + core * 8 + y * 2, 2)], own_sem.at[0]
    )
    mine.start()
    for copy in loads[2:]:
        copy.wait()
    for d in range(1, SIDE):
        index(d).start()
    for b in range(2):
        tokens = pl.ds(b * BLOCK, BLOCK)
        units = pl.ds(b * heads, heads)
        qd[units, 0] = jnp.swapaxes(q[tokens], 0, 1)
        qd[units, 1] = jnp.swapaxes(g[tokens], 0, 1)
    mine.wait()
    for d in range(1, SIDE):
        near(d).wait_recv()
    first(2 - outer, 2 * (2 * parity + 2 - y)).start()
    first(1, 2 * (parity + 1)).start()
    share_own(core).start()

    def send_query(i, carry):
        query(i).start()
        return carry

    lax.fori_loop(1, PLANE, send_query, 0)
    qd_out[x * SIDE + y] = qd[unit_of(x, y)]
    sel_all[x] = sel[...]
    share_own(1 - core).wait_recv()
    for i in range(3):
        hop(1, 1, i).start()

    def clear(i, carry):
        acc[pl.ds(i * 4, 4)] = jnp.zeros((4, 2, BLOCK, HEAD), jnp.bfloat16)
        return carry

    lax.fori_loop(0, acc.shape[0] // 4, clear, 0)

    def retire(j):
        for k in range(2):
            for i in range(3):
                hop(j, k, i).wait_send()
                shared(j, k, i).wait_recv()
                share(j, k, i).wait_send()
            cross(j, k).wait_send()
            overed(j, k).wait_recv()
            over(j, k).wait_send()

    def step(s, carry):
        for k in range(2):
            for i in range(3):
                arrived(s - 1, k, i).wait_recv()
                hop(s, k, i).start()
                if i == 0:
                    cross(s - 1, k).start()
                share(s - 1, k, i).start()

        @pl.when(s > 2)
        def _():
            for k in range(2):
                crossed(s - 2, k).wait_recv()
                over(s - 2, k).start()

        @pl.when(s > 4)
        def _():
            retire(s - 4)

        return carry

    lax.fori_loop(2, half_way, step, 0)
    def finish_query(i, carry):
        query(i).wait()
        return carry

    lax.fori_loop(1, PLANE, finish_query, 0)
    for d in range(1, SIDE):
        index(d).wait()
    own_head = lax.broadcasted_iota(jnp.int32, sel.shape, 1) == 2 * x + y // 2
    for group in range(SIDE):
        sel_out[group] = jnp.sum(jnp.where(own_head, sel_all[group], 0), axis=1)
    for d in range(1, SIDE):
        near(d).wait_send()
    share_own(core).wait_send()
    retire(last - 3)
    for k in range(2):
        for i in range(3):
            arrived(last, k, i).wait_recv()
            if k == 0:
                hop(half_way, 0, i).start()
            if i == 0:
                cross(last, k).start()
            share(last, k, i).start()
    for k in range(2):
        crossed(last - 1, k).wait_recv()
        over(last - 1, k).start()
    retire(last - 2)
    for i in range(3):
        arrived(half_way, 0, i).wait_recv()
        if i == 0:
            cross(half_way, 0).start()
            cross_over(6 * parity, core).start()
        share(half_way, 0, i).start()
    for k in range(2):
        crossed(last, k).wait_recv()
        over(last, k).start()

    retire(last - 1)
    retire(last)
    for i in range(3):
        hop(half_way, 0, i).wait_send()
        shared(half_way, 0, i).wait_recv()
        share(half_way, 0, i).wait_send()
    cross(half_way, 0).wait_send()
    cross_over(6 * parity, core).wait_send()
    crossed(half_way, 0).wait_recv()
    cross_over(6 * (1 - parity), 1 - core).wait_recv()


def attend(sel, qd, store, cleared, od, acc):
    x, y, z, core = place()
    parity = y % 2
    factor = HEAD**-0.5
    rate = factor * math.log2(math.e)
    f32, bf16 = jnp.float32, jnp.bfloat16
    nt = (((1,), (1,)), ((), ()))
    nn = (((1,), (0,)), ((), ()))
    tn = (((0,), (0,)), ((), ()))

    def dot(a, b, dims):
        return lax.dot_general(a, b, dims, preferred_element_type=f32)

    def one(side, carry):
        own = z * 16 + core * 8 + side * 2 + parity
        block = ((z * SIDE + side) * 2 + core) * 2 + parity
        own_terms = [jnp.zeros((BLOCK, HEAD), f32)] * 2
        groups = range(SIDE)
        rows, keys, values = {}, {}, {}
        for group in groups:
            rows[group] = [own]
            for t in range(3):
                n = sel[group, t, block]
                rows[group].append(
                    (n // 16) * 16 + ((n // 2) % 2) * 8 + ((n // 4) % SIDE) * 2 + n % 2
                )
        for group in groups:
            keys[group] = jnp.concatenate([store[r, 0] for r in rows[group]], axis=0)
            values[group] = jnp.concatenate([store[r, 1] for r in rows[group]], axis=0)
        q = {group: qd[group * SIDE + side, 0] for group in groups}
        g = {group: qd[group * SIDE + side, 1] for group in groups}
        scores = {group: dot(q[group], keys[group], nt) for group in groups}
        grad_prob = {group: dot(g[group], values[group], nt) for group in groups}
        top = {group: jnp.max(scores[group], axis=1, keepdims=True) for group in groups}
        e = {group: jnp.exp2((scores[group] - top[group]) * rate) for group in groups}
        total = {group: jnp.sum(e[group], axis=1, keepdims=True) for group in groups}
        inverse = {group: 1.0 / total[group] for group in groups}
        prob_b = {group: (e[group] * inverse[group]).astype(bf16) for group in groups}
        scaled = {group: e[group] * (inverse[group] * factor) for group in groups}
        out = {group: dot(prob_b[group], values[group], nn).astype(bf16) for group in groups}
        value_terms = {group: dot(prob_b[group], g[group], tn) for group in groups}
        delta = {
            group: jnp.sum(g[group].astype(f32) * out[group].astype(f32), axis=1, keepdims=True)
            for group in groups
        }
        grad_scores = {
            group: (scaled[group] * (grad_prob[group] - delta[group])).astype(bf16)
            for group in groups
        }
        key_terms = {group: dot(grad_scores[group], q[group], tn) for group in groups}
        query_terms = {group: dot(grad_scores[group], keys[group], nn) for group in groups}
        for group in groups:
            u = group * SIDE + side
            od[u, 0] = out[group]
            od[u, 1] = query_terms[group].astype(bf16)
            for i, terms in enumerate((key_terms[group], value_terms[group])):
                own_terms[i] += terms[:BLOCK]
                for t in range(1, 4):
                    row = rows[group][t]
                    part = terms[t * BLOCK : (t + 1) * BLOCK]
                    acc[row, i] = (acc[row, i].astype(f32) + part).astype(bf16)
        for i in range(2):
            acc[own, i] = (acc[own, i].astype(f32) + own_terms[i]).astype(bf16)
        return carry

    lax.fori_loop(0, SIDE, one, 0)


def give(
    planes,
    od,
    acc,
    att,
    grad_q,
    kvg,
    part,
    inbox,
    outbox,
    mate_in,
    mate_out,
    fin,
    spread,
    od_all,
    q_send,
    q_recv,
    pair_send,
    pair_recv,
    mate_send,
    mate_recv,
    ring_send,
    ring_recv,
    near_send,
    near_recv,
    mine_sem,
):
    x, y, z, core = place()
    half_way = planes // 2
    parity = y % 2
    mate = y + 1 - 2 * parity
    heads = att.shape[1]
    f32, bf16 = jnp.float32, jnp.bfloat16

    announce(planes, x, y, z, core)
    for d in range(2):
        inbox[d, 0, 1, 1 - d] = jnp.zeros((2, BLOCK, HEAD), bf16)
    all_here()

    def chunk(d, s):
        far = half_way - s
        return (z + far) % planes if d == 0 else (z + planes - far) % planes

    def pair(at):
        return remote(
            acc.at[pl.ds(at * 16 + (1 - core) * 8, 8)],
            part.at[at],
            pair_send.at[at],
            pair_recv.at[at],
            ctx_of(z, y, 1 - core),
            x,
        )

    def cross(at):
        return remote(
            mate_out.at[at],
            mate_in.at[at],
            mate_send.at[at],
            mate_recv.at[at],
            ctx_of(z, mate, core),
            x,
        )

    def hop(d, s, i):
        to = (z + 1) % planes if d == 0 else (z + planes - 1) % planes
        box = (d, s, i, pl.ds(d, 1)) if isinstance(s, int) and s == 0 and i == 1 else (d, s, i)
        return remote(
            outbox.at[box],
            inbox.at[box],
            ring_send.at[d, s, i],
            ring_recv.at[d, s, i],
            ctx_of(to, y, core),
            x,
        )

    def answer(i):
        t = (x * SIDE + y + i) % PLANE
        return remote(
            od.at[t],
            od_all.at[unit_of(x, y)],
            q_send.at[i - 1],
            q_recv.at[i - 1],
            ctx_of(z, t % SIDE, core),
            t // SIDE,
        )

    def near(d):
        to = (y + d) % SIDE
        return remote(
            fin.at[pl.ds(to * 2, 2)],
            spread.at[y],
            near_send.at[d - 1],
            near_recv.at[d - 1],
            ctx_of(z, to, core),
            x,
        )

    def chip_sum(at, first, count):
        mine = acc[pl.ds(at * 16 + core * 8 + first, count)].astype(f32)
        return mine + part[at, pl.ds(first, count)].astype(f32)

    def prepare(at):
        pair(at).wait_recv()
        mate_out[at] = chip_sum(at, 6 * (1 - parity), 2).astype(bf16)
        cross(at).start()

    def emit(d, s, i, extra):
        at = chunk(d, s)
        total = chip_sum(at, 2 * piece_of(parity, i), 2)
        if i == 0:
            total += mate_in[at].astype(f32)
        if extra:
            hop(d, s - 1, i).wait_recv()
            total += inbox[d, s - 1, i].astype(f32)
        outbox[d, s, i] = total.astype(bf16)
        hop(d, s, i).start()

    pair(chunk(0, 0)).start()

    def begin_step(s, carry):
        pair(chunk(0, s)).start()
        pair(chunk(1, s)).start()
        return carry

    begin_step(1, 0)

    prepare(chunk(0, 0))
    for d in range(2):
        emit(d, 0, 1, False)
    emit(1, 0, 2, False)
    lax.fori_loop(2, half_way, begin_step, 0)
    pair(z).start()
    home = pltpu.make_async_copy(od.at[x * SIDE + y], od_all.at[unit_of(x, y)], mine_sem)
    home.start()
    for d in range(2):
        prepare(chunk(d, 1))
    cross(chunk(0, 0)).wait_recv()
    emit(0, 0, 0, False)
    for d in range(2):
        prepare(chunk(d, 2))
    for i in (2, 1, 0):
        for d in range(2):
            if i == 0:
                cross(chunk(d, 1)).wait_recv()
            emit(d, 1, i, i in HALVES[d])

    each = (PLANE - 1) // (half_way - 3)

    def step(s, carry):
        @pl.when(s + 1 < half_way)
        def _():
            for d in range(2):
                prepare(chunk(d, s + 1))
            for i in range(1, 1 + each):
                answer((s - 2) * each + i).start()

        for i in (2, 1, 0):
            for d in range(2):
                if i == 0:
                    cross(chunk(d, s)).wait_recv()
                emit(d, s, i, True)
        return carry

    lax.fori_loop(2, half_way, step, 0)

    def scatter(to):
        @pl.when(to != y)
        def _():
            near((to + SIDE - y) % SIDE).start()

    pair(z).wait_recv()
    rest = 6 * (1 - parity)
    fin[pl.ds(rest, 2)] = chip_sum(z, rest, 2).astype(bf16)
    scatter(3 * (1 - parity))

    def finish_answer(i, carry):
        answer(i).wait()
        return carry

    lax.fori_loop(1, PLANE, finish_answer, 0)
    home.wait()
    for b in range(2):
        tokens = pl.ds(b * BLOCK, BLOCK)
        units = pl.ds(b * heads, heads)
        att[tokens] = jnp.swapaxes(od_all[units, 0], 0, 1)
        grad_q[tokens] = jnp.swapaxes(od_all[units, 1], 0, 1)

    for i in (2, 1, 0):
        first = 2 * piece_of(parity, i)
        total = chip_sum(z, first, 2)
        for d in range(2):
            hop(d, half_way - 1, i).wait_recv()
            total += inbox[d, half_way - 1, i].astype(f32)
        fin[pl.ds(first, 2)] = total.astype(bf16)
        scatter(piece_of(parity, i))
    spread[y] = fin[pl.ds(y * 2, 2)]

    def finish(s, carry):
        for d in range(2):
            for i in range(3):
                hop(d, s, i).wait_send()
            cross(chunk(d, s)).wait_send()
            pair(chunk(d, s)).wait_send()
        return carry

    lax.fori_loop(1, half_way, finish, 0)
    for d in range(2):
        for i in HALVES[d]:
            hop(d, 0, i).wait_send()
    cross(chunk(0, 0)).wait_send()
    pair(chunk(0, 0)).wait_send()
    pair(z).wait_send()

    for d in range(1, SIDE):
        near(d).wait()
    for pick in range(2):
        kvg[pick] = (spread[2 * pick].astype(f32) + spread[2 * pick + 1].astype(f32)).astype(bf16)


def leave(att, grad_q, kvg, att_out, grad_q_out, grad_k_out, grad_v_out, pair, sem):
    copies = [
        pltpu.make_async_copy(src, dst, sem.at[i])
        for i, (src, dst) in enumerate(
            (
                (att, att_out),
                (grad_q, grad_q_out),
                (pair.at[0], grad_k_out),
                (pair.at[1], grad_v_out),
            )
        )
    ]
    for copy in copies[:2]:
        copy.start()
    for b in range(2):
        for i in range(2):
            pair[i, pl.ds(b * BLOCK, BLOCK)] = jnp.swapaxes(kvg[:, b, i], 0, 1)
    for copy in copies[2:]:
        copy.start()
    for copy in copies:
        copy.wait()


def local(planes, queries, key_states, value_states, grad_out, selected):
    bf16 = jnp.bfloat16
    dma = pltpu.SemaphoreType.DMA
    half_way = planes // 2
    heads = queries.shape[1]
    blocks = selected.shape[0]

    shape = jax.ShapeDtypeStruct
    units = (PLANE, 2, BLOCK, HEAD)
    rows = (planes * 16, 2, BLOCK, HEAD)
    lists = (3, heads, blocks)
    given = queries, grad_out, key_states, value_states, selected.transpose(2, 1, 0)

    qd, sel, store, cleared = pl.pallas_call(
        functools.partial(bring, planes),
        name="bring",
        out_shape=(
            shape(units, bf16),
            shape((SIDE, 3, blocks), jnp.int32),
            shape(rows, bf16),
            shape(rows, bf16),
        ),
        in_specs=[HBM] * 5,
        out_specs=(VMEM,) * 4,
        scratch_shapes=[
            pltpu.VMEM(queries.shape, bf16),
            pltpu.VMEM(queries.shape, bf16),
            pltpu.VMEM(queries.shape, bf16),
            pltpu.VMEM(queries.shape, bf16),
            pltpu.VMEM(lists, jnp.int32),
            pltpu.VMEM(units, bf16),
            pltpu.VMEM((heads, 2, 2, BLOCK, HEAD), bf16),
            pltpu.VMEM((SIDE, *lists), jnp.int32),
            dma((5,)),
            dma((SIDE - 1,)),
            dma((SIDE - 1,)),
            dma((PLANE - 1,)),
            dma((PLANE - 1,)),
            dma((SIDE - 1,)),
            dma((SIDE - 1,)),
            dma((half_way, 2, 3)),
            dma((half_way, 2, 3)),
            dma((half_way, 2, 3)),
            dma((half_way, 2, 3)),
            dma((half_way, 2)),
            dma((half_way, 2)),
            dma((half_way, 2)),
            dma((half_way, 2)),
            dma((3,)),
        ],
        compiler_params=pltpu.CompilerParams(
            collective_id=0, has_side_effects=True, vmem_limit_bytes=16 * 1024 * 1024
        ),
    )(*(pltpu.with_memory_space_constraint(a, pltpu.HBM) for a in given))

    od, acc = pl.pallas_call(
        attend,
        name="attend",
        out_shape=(shape(units, bf16), shape(rows, bf16)),
        in_specs=[SMEM, VMEM, VMEM, VMEM],
        out_specs=(VMEM, VMEM),
        input_output_aliases={3: 1},
        compiler_params=pltpu.CompilerParams(vmem_limit_bytes=24 * 1024 * 1024),
    )(sel, qd, store, cleared)

    piece = (3, 2, 2, BLOCK, HEAD)
    att, grad_q, kvg = pl.pallas_call(
        functools.partial(give, planes),
        name="give",
        out_shape=(
            shape(queries.shape, bf16),
            shape(queries.shape, bf16),
            shape((2, 2, 2, BLOCK, HEAD), bf16),
        ),
        in_specs=[VMEM, VMEM],
        out_specs=(VMEM,) * 3,
        scratch_shapes=[
            pltpu.VMEM((planes, 8, 2, BLOCK, HEAD), bf16),
            pltpu.VMEM((2, half_way, *piece), bf16),
            pltpu.VMEM((2, half_way, *piece), bf16),
            pltpu.VMEM((planes, 2, 2, BLOCK, HEAD), bf16),
            pltpu.VMEM((planes, 2, 2, BLOCK, HEAD), bf16),
            pltpu.VMEM((8, 2, BLOCK, HEAD), bf16),
            pltpu.VMEM((SIDE, 2, 2, BLOCK, HEAD), bf16),
            pltpu.VMEM(units, bf16),
            dma((PLANE - 1,)),
            dma((PLANE - 1,)),
            dma((planes,)),
            dma((planes,)),
            dma((planes,)),
            dma((planes,)),
            dma((2, half_way, 3)),
            dma((2, half_way, 3)),
            dma((SIDE - 1,)),
            dma((SIDE - 1,)),
            dma,
        ],
        compiler_params=pltpu.CompilerParams(
            collective_id=1, has_side_effects=True, vmem_limit_bytes=28 * 1024 * 1024
        ),
    )(od, acc)

    key_shape = (2 * BLOCK, 2, HEAD)
    return pl.pallas_call(
        leave,
        name="leave",
        out_shape=(
            shape(queries.shape, bf16),
            shape(queries.shape, bf16),
            shape(key_shape, bf16),
            shape(key_shape, bf16),
        ),
        in_specs=[VMEM] * 3,
        out_specs=(HBM,) * 4,
        scratch_shapes=[pltpu.VMEM((2, *key_shape), bf16), dma((4,))],
        compiler_params=pltpu.CompilerParams(vmem_limit_bytes=4 * 1024 * 1024),
    )(att, grad_q, kvg)


def solution(mesh):
    planes = mesh.shape["ctx"] // (2 * SIDE)
    spread = P("ctx", "head", None)
    whole = P("ctx", None, None)
    return jax.shard_map(
        functools.partial(local, planes),
        mesh=mesh,
        in_specs=(spread, whole, whole, spread, P(None, "head", None)),
        out_specs=(spread, spread, spread, spread),
        check_vma=False,
    )
```
